32 devices in a mesh: shard: 4 (over y, x), replica: 8 (over z, core).
Axes of the slice: x: 2, y: 2, z: 4, core: 2. Of those that a mesh axis runs over, the one named last changes fastest.
Arguments:
- tokens: bfloat16 [8192, 768], P(('shard', 'replica')), may hold values from -6 to 6
- cond: bfloat16 [32, 768], P(('shard', 'replica')), may hold values from -6 to 6
- cot: bfloat16 [8192, 768], P(('shard', 'replica')), may hold values from -6 to 6
- w_mod: bfloat16 [768, 4608], P('shard'), may hold values from -0.21875 to 0.21875
- b_mod: bfloat16 [4608], P('shard'), may hold values from -2.5 to 2.5
- w_qkv: bfloat16 [768, 2304], P('shard'), may hold values from -0.21875 to 0.21875
- b_qv: bfloat16 [1536], P('shard'), may hold values from -2.5 to 2.5
- w_out: bfloat16 [768, 768], P('shard'), may hold values from -0.875 to 0.875
- b_out: bfloat16 [768], P('shard'), may hold values from -2.5 to 2.5
- w_fc1: bfloat16 [768, 3072], P('shard'), may hold values from -0.21875 to 0.21875
- b_fc1: bfloat16 [3072], P('shard'), may hold values from -2.5 to 2.5
- w_fc2: bfloat16 [3072, 768], P('shard'), may hold values from -0.109375 to 0.109375
- b_fc2: bfloat16 [768], P('shard'), may hold values from -2.5 to 2.5
Outputs:
- mixed: bfloat16 [8192, 768], P(('shard', 'replica'))
- grad_tokens: float32 [8192, 768], P(('shard', 'replica'))
- grad_cond: float32 [32, 768], P(('shard', 'replica'))
- grad_w_mod: float32 [768, 4608], P('shard')
- grad_b_mod: float32 [4608], P('shard')
- grad_w_qkv: float32 [768, 2304], P('shard')
- grad_b_qv: float32 [1536], P('shard')
- grad_w_out: float32 [768, 768], P('shard')
- grad_b_out: float32 [768], P('shard')
- grad_w_fc1: float32 [768, 3072], P('shard')
- grad_b_fc1: float32 [3072], P('shard')
- grad_w_fc2: float32 [3072, 768], P('shard')
- grad_b_fc2: float32 [768], P('shard')
The draws below stay inside these ranges and needn't reach their ends.
All inputs are finite; a program needn't handle non-finite values.
Results may differ from the reference program's by a relative error of at most 0.015.
The reference program's roundings to bfloat16 on the way count: a program that leaves them out, or rounds other values in their place, can miss the bound.
Values may be sent and summed in bfloat16 or wider, within the bound.
No kernel may reach another device: no remote copies, remote signals or barrier semaphores. Data moves between devices by JAX's collectives and lax.ppermute only.
A program may use at most 192 MiB of HBM per device.

```python
import math
import jax
import jax.numpy as jnp
from jax import lax

D = 768
FF = 3072
LAT_TOK = 256
LATENTS = 32
TOKENS = 8192


def block_levels(key, dims, cuts, low, top_value):
    def one(axis_at, blocks):
        draws = jax.random.uniform(jax.random.fold_in(jax.random.fold_in(key, 6), axis_at), (blocks,), jnp.float32, low / len(cuts), top_value / len(cuts))
        return jnp.repeat(jnp.exp(draws), dims[axis_at] // blocks).reshape((-1,) + (1,) * (len(dims) - axis_at - 1))

    loudness = one(*cuts[0])
    for cut in cuts[1:]:
        loudness = loudness * one(*cut)
    return loudness


def gaussian(stream_key, dims, deviation, bound, cuts=(), dtype=jnp.bfloat16):
    drawn = jax.random.normal(stream_key, dims, jnp.float32) * deviation
    if len(cuts) > 0:
        drawn = block_levels(stream_key, dims, cuts, -0.22, 0.18) * drawn
    return jnp.clip(drawn, min=-bound, max=bound).astype(dtype)


def setup_inputs(seed: int = 0) -> dict:
    splits = jax.random.split(jax.random.key(seed), 14)
    tokens = gaussian(splits[0], (TOKENS, D), 1.0, 6.0, ((0, 32),))
    cond = gaussian(splits[1], (LATENTS, D), 1.0, 6.0, ((0, 32),))
    cot = gaussian(splits[2], (TOKENS, D), 1.0, 6.0, ((0, 32),))
    w_mod = gaussian(splits[3], (D, 6 * D), D ** -0.5, 0.21875, ((0, 4),))
    b_mod = gaussian(splits[4], (6 * D,), 0.4, 2.5, ((0, 4),))
    w_qkv = gaussian(splits[5], (D, 3 * D), D ** -0.5, 0.21875, ((0, 4),))
    b_qv = gaussian(splits[6], (2 * D,), 0.4, 2.5, ((0, 4),))
    w_out = gaussian(splits[7], (D, D), (D // 16) ** -0.5, 0.875, ((0, 4),))
    b_out = gaussian(splits[8], (D,), 0.4, 2.5, ((0, 4),))
    w_fc1 = gaussian(splits[9], (D, FF), D ** -0.5, 0.21875, ((0, 4),))
    b_fc1 = gaussian(splits[10], (FF,), 0.4, 2.5, ((0, 4),))
    w_fc2 = gaussian(splits[11], (FF, D), FF ** -0.5, 0.109375, ((0, 4),))
    b_fc2 = gaussian(splits[12], (D,), 0.4, 2.5, ((0, 4),))
    return dict(tokens=tokens, cond=cond, cot=cot, w_mod=w_mod, b_mod=b_mod, w_qkv=w_qkv, b_qv=b_qv, w_out=w_out, b_out=b_out, w_fc1=w_fc1, b_fc1=b_fc1, w_fc2=w_fc2, b_fc2=b_fc2)


def matmul(left, right):
    return jnp.dot(left, right, preferred_element_type=jnp.float32)

def matmul_tn(left, right):
    return lax.dot_general(left, right, (((0,), (0,)), ((), ())), preferred_element_type=jnp.float32)

def matmul_nt(left, right):
    return lax.dot_general(left, right, (((1,), (1,)), ((), ())), preferred_element_type=jnp.float32)

def batched(form, left, right):
    return jnp.einsum(form, left.astype(jnp.float32), right.astype(jnp.float32), precision=lax.Precision.HIGHEST)

def layer_norm(values):
    center = values - lax.optimization_barrier(jnp.mean(values, -1, keepdims=True))
    rstd_val = lax.rsqrt(lax.optimization_barrier(jnp.mean(center * center, -1, keepdims=True)) + 1e-06)
    return (center * rstd_val, rstd_val)

def norm_back(grad_norm, normed, rstd_val):
    return rstd_val * (grad_norm - lax.optimization_barrier(jnp.mean(grad_norm, -1, keepdims=True)) - normed * lax.optimization_barrier(jnp.mean(grad_norm * normed, -1, keepdims=True)))

def gelu_tanh(pre_value):
    return jax.nn.gelu(pre_value, approximate=True)

def block_pass(tokens, cond, cot, weights, fetch_back):
    w_mod, b_mod, w_qkv, b_qv, w_out, b_out, w_fc1, b_fc1, w_fc2, b_fc2 = weights
    latent_count, token_count, model_width = tokens.shape
    head_count = model_width // 64
    row_count = latent_count * token_count
    cond_f = cond.astype(jnp.float32)
    cond_act = jax.nn.silu(cond_f).astype(jnp.bfloat16)
    modulation = matmul(cond_act, w_mod) + b_mod.astype(jnp.float32)
    pieces = [modulation[:, offset * model_width:(offset + 1) * model_width][:, None, :] for offset in range(6)]
    shift_a, scale_a, gate_a, shift_b, scale_b, gate_b = pieces
    inputs = tokens.astype(jnp.float32)
    norm_a, rstd_a = layer_norm(inputs)
    modul_a = (norm_a * (1.0 + scale_a) + shift_a).astype(jnp.bfloat16).reshape(row_count, model_width)
    projected = matmul(modul_a, w_qkv)
    bias_qv = b_qv.astype(jnp.float32)
    head_shape = (latent_count, token_count, head_count, 64)
    queries = (projected[:, :model_width] + bias_qv[:model_width]).astype(jnp.bfloat16).reshape(head_shape)
    keys_b = projected[:, model_width:2 * model_width].astype(jnp.bfloat16).reshape(head_shape)
    values_b = (projected[:, 2 * model_width:] + bias_qv[model_width:]).astype(jnp.bfloat16).reshape(head_shape)
    scores = batched('lqhd,lkhd->lhqk', queries, keys_b) * 0.125
    row_max = lax.optimization_barrier(jnp.max(scores, -1, keepdims=True))
    exp_scores = jnp.exp(scores - row_max)
    row_total = lax.optimization_barrier(jnp.sum(exp_scores, -1, keepdims=True))
    log_total = row_max + jnp.log(row_total)
    attn_probs = (exp_scores / row_total).astype(jnp.bfloat16)
    attended = batched('lhqk,lkhd->lqhd', attn_probs, values_b).astype(jnp.bfloat16)
    attn_flat = attended.reshape(row_count, model_width)
    branch_a = (matmul(attn_flat, w_out) + b_out.astype(jnp.float32)).reshape(latent_count, token_count, model_width)
    middle = inputs + gate_a * branch_a
    norm_b, rstd_b = layer_norm(middle)
    modul_b = (norm_b * (1.0 + scale_b) + shift_b).astype(jnp.bfloat16).reshape(row_count, model_width)
    hidden_pre = matmul(modul_b, w_fc1) + b_fc1.astype(jnp.float32)
    hidden = gelu_tanh(hidden_pre).astype(jnp.bfloat16)
    branch_b = (matmul(hidden, w_fc2) + b_fc2.astype(jnp.float32)).reshape(latent_count, token_count, model_width)
    output = (middle + gate_b * branch_b).astype(jnp.bfloat16)
    back_mod, back_qkv, back_out, back_fc1, back_fc2 = fetch_back()
    grad_out = cot.astype(jnp.float32)
    grad_gate_b = lax.optimization_barrier(jnp.sum(grad_out * branch_b, 1))
    grad_branch_b = (grad_out * gate_b).reshape(row_count, model_width)
    branch_b_low = grad_branch_b.astype(jnp.bfloat16)
    grad_w_fc2 = matmul_tn(hidden, branch_b_low)
    grad_b_fc2 = lax.optimization_barrier(jnp.sum(grad_branch_b, 0))
    grad_hidden = matmul_nt(branch_b_low, back_fc2)
    gelu_value, gelu_back = jax.vjp(gelu_tanh, hidden_pre)
    grad_pre = gelu_back(grad_hidden)[0]
    grad_pre_low = grad_pre.astype(jnp.bfloat16)
    grad_w_fc1 = matmul_tn(modul_b, grad_pre_low)
    grad_b_fc1 = lax.optimization_barrier(jnp.sum(grad_pre, 0))
    grad_modul_b = matmul_nt(grad_pre_low, back_fc1).reshape(latent_count, token_count, model_width)
    grad_shift_b = lax.optimization_barrier(jnp.sum(grad_modul_b, 1))
    grad_scale_b = lax.optimization_barrier(jnp.sum(grad_modul_b * norm_b, 1))
    grad_middle = grad_out + norm_back(grad_modul_b * (1.0 + scale_b), norm_b, rstd_b)
    grad_gate_a = lax.optimization_barrier(jnp.sum(grad_middle * branch_a, 1))
    grad_branch_a = (grad_middle * gate_a).reshape(row_count, model_width)
    branch_a_low = grad_branch_a.astype(jnp.bfloat16)
    grad_w_out = matmul_tn(attn_flat, branch_a_low)
    grad_b_out = lax.optimization_barrier(jnp.sum(grad_branch_a, 0))
    grad_attended = matmul_nt(branch_a_low, back_out).astype(jnp.bfloat16).reshape(head_shape)
    again_scores = batched('lqhd,lkhd->lhqk', queries, keys_b) * 0.125
    again_probs = jnp.exp(again_scores - log_total)
    grad_values = batched('lhqk,lqhd->lkhd', again_probs.astype(jnp.bfloat16), grad_attended)
    grad_probs = batched('lqhd,lkhd->lhqk', grad_attended, values_b)
    delta_rows = batched('lqhd,lqhd->lhq', grad_attended, attended)
    grad_scores = (again_probs * (grad_probs - delta_rows[..., None]) * 0.125).astype(jnp.bfloat16)
    grad_queries = batched('lhqk,lkhd->lqhd', grad_scores, keys_b)
    grad_keys = batched('lhqk,lqhd->lkhd', grad_scores, queries)
    grad_proj = jnp.concatenate([grad_queries.reshape(row_count, model_width), grad_keys.reshape(row_count, model_width), grad_values.reshape(row_count, model_width)], 1)
    grad_proj_low = grad_proj.astype(jnp.bfloat16)
    grad_w_qkv = matmul_tn(modul_a, grad_proj_low)
    grad_b_qv = jnp.concatenate([lax.optimization_barrier(jnp.sum(grad_proj[:, :model_width], 0)), lax.optimization_barrier(jnp.sum(grad_proj[:, 2 * model_width:], 0))])
    grad_modul_a = matmul_nt(grad_proj_low, back_qkv).reshape(latent_count, token_count, model_width)
    grad_shift_a = lax.optimization_barrier(jnp.sum(grad_modul_a, 1))
    grad_scale_a = lax.optimization_barrier(jnp.sum(grad_modul_a * norm_a, 1))
    grad_inputs = grad_middle + norm_back(grad_modul_a * (1.0 + scale_a), norm_a, rstd_a)
    grad_modulation = jnp.concatenate([grad_shift_a, grad_scale_a, grad_gate_a, grad_shift_b, grad_scale_b, grad_gate_b], 1)
    grad_mod_low = grad_modulation.astype(jnp.bfloat16)
    grad_w_mod = matmul_tn(cond_act, grad_mod_low)
    grad_b_mod = lax.optimization_barrier(jnp.sum(grad_modulation, 0))
    grad_cond_act = matmul_nt(grad_mod_low, back_mod)
    silu_value, silu_back = jax.vjp(jax.nn.silu, cond_f)
    grad_cond = silu_back(grad_cond_act)[0]
    grads = (grad_w_mod, grad_b_mod, grad_w_qkv, grad_b_qv, grad_w_out, grad_b_out, grad_w_fc1, grad_b_fc1, grad_w_fc2, grad_b_fc2)
    return (output, grad_inputs, grad_cond, grads)

def reference(tokens, cond, cot, w_mod, b_mod, w_qkv, b_qv, w_out, b_out, w_fc1, b_fc1, w_fc2, b_fc2):
    weights = (w_mod, b_mod, w_qkv, b_qv, w_out, b_out, w_fc1, b_fc1, w_fc2, b_fc2)
    back_set = (w_mod, w_qkv, w_out, w_fc1, w_fc2)
    group_size = math.gcd(LATENTS, 16)
    group_count = LATENTS // group_size
    token_blocks = tokens.reshape(group_count, group_size, LAT_TOK, D)
    cond_blocks = cond.reshape(group_count, group_size, D)
    cot_blocks = cot.reshape(group_count, group_size, LAT_TOK, D)

    def scan_step(running, inputs_blk):
        token_blk, cond_blk, cot_blk = inputs_blk
        output, grad_inputs, grad_cond, grads = block_pass(token_blk, cond_blk, cot_blk, weights, lambda: back_set)
        running = tuple((total_val + grad_val for total_val, grad_val in zip(running, grads)))
        return (running, (output, grad_inputs, grad_cond))
    start = tuple((jnp.zeros(weight.shape, jnp.float32) for weight in weights))
    totals, stacked = lax.scan(scan_step, start, (token_blocks, cond_blocks, cot_blocks))
    mixed = stacked[0].reshape(TOKENS, D)
    grad_tokens = stacked[1].reshape(TOKENS, D)
    grad_cond = stacked[2].reshape(LATENTS, D)
    return (mixed, grad_tokens, grad_cond, totals[0], totals[1], totals[2], totals[3], totals[4], totals[5], totals[6], totals[7], totals[8], totals[9])
```

```python
import jax
import jax.numpy as jnp
from jax import lax
from jax.sharding import PartitionSpec as P

F32 = jnp.float32
BF16 = jnp.bfloat16


def matmul(left, right):
    return jnp.dot(left, right, preferred_element_type=F32)


def matmul_tn(left, right):
    return lax.dot_general(left, right, (((0,), (0,)), ((), ())), preferred_element_type=F32)


def matmul_nt(left, right):
    return lax.dot_general(left, right, (((1,), (1,)), ((), ())), preferred_element_type=F32)


def batched(form, left, right):
    return jnp.einsum(form, left, right, preferred_element_type=F32)


def layer_norm(values):
    center = values - jnp.mean(values, -1, keepdims=True)
    rstd_val = lax.rsqrt(jnp.mean(center * center, -1, keepdims=True) + 1e-06)
    return (center * rstd_val, rstd_val)


def norm_back(grad_norm, normed, rstd_val):
    return rstd_val * (
        grad_norm
        - jnp.mean(grad_norm, -1, keepdims=True)
        - normed * jnp.mean(grad_norm * normed, -1, keepdims=True)
    )


def gelu_tanh(pre_value):
    return jax.nn.gelu(pre_value, approximate=True)


def hop(value, axis, size, flip):
    return lax.ppermute(value, axis, [(at, at ^ flip) for at in range(size)])


def bits_of(number):
    return [1 << at for at in range(number.bit_length()) if number >> at & 1]


def by_weight(count):
    return sorted(range(1, count), key=lambda number: (bin(number).count("1"), number))


def xor_rows(rows, place):
    count = rows.shape[0]
    flip = 1
    while flip < count:
        swapped = rows.reshape(count // (2 * flip), 2, flip, -1)[:, ::-1].reshape(rows.shape)
        rows = jnp.where((place & flip) != 0, swapped, rows)
        flip *= 2
    return rows


def gather_weight(weight, core, shards):
    half_rows = weight.shape[0] // 2
    width = weight.shape[1]
    mine = {0: lax.dynamic_slice_in_dim(weight, core * half_rows, half_rows, 0)}
    theirs = {}
    for number in by_weight(shards):
        ways = bits_of(number)
        part = width // len(ways)
        got = [
            hop(mine[number ^ flip][:, at * part : (at + 1) * part], "shard", shards, flip)
            for at, flip in enumerate(ways)
        ]
        mine[number] = got[0] if len(got) == 1 else jnp.concatenate(got, 1)
    return mine, theirs


def join_weight(weight, mine, replicas, shards):
    rows = [weight]
    for number in range(1, shards):
        rows += [mine[number], hop(mine[number], "replica", replicas, 1)]
    return jnp.concatenate(rows, 0)


def reduce_grad(grad, core, shards, replicas):
    rows, width = grad.shape
    block = rows // shards
    half = block // 2
    low = grad.astype(BF16).reshape(shards, 2, half, width)
    own = low[0]
    own_keep = lax.dynamic_slice_in_dim(own, core, 1, 0)
    own_send = lax.dynamic_slice_in_dim(own, 1 - core, 1, 0)
    keep = jnp.concatenate([own_keep, low[1:, 0]], 0)
    send = jnp.concatenate([own_send, low[1:, 1]], 0)
    came = hop(send, "replica", replicas, 1)
    total = keep.astype(F32) + came.astype(F32)
    parts = {number: total[number] for number in range(shards)}
    for number in reversed(by_weight(shards)):
        ways = bits_of(number)
        part = width // len(ways)
        for at, flip in enumerate(ways):
            got = hop(
                parts[number][:, at * part : (at + 1) * part].astype(BF16), "shard", shards, flip
            ).astype(F32)
            target = number ^ flip
            if len(ways) == 1:
                parts[target] = parts[target] + got
            else:
                edges = [parts[target][:, : at * part], parts[target][:, (at + 1) * part :]]
                parts[target] = jnp.concatenate(
                    [edges[0], parts[target][:, at * part : (at + 1) * part] + got, edges[1]], 1
                )
    value = parts[0]
    flips = []
    flip = 2
    place = lax.axis_index("replica")
    while flip < replicas:
        span = value.shape[1] // 2
        high = (place & flip) != 0
        sent = jnp.where(high, value[:, :span], value[:, span:]).astype(BF16)
        kept = jnp.where(high, value[:, span:], value[:, :span])
        value = kept + hop(sent, "replica", replicas, flip).astype(F32)
        flips.append(flip)
        flip *= 2
    value = value.astype(BF16)
    for flip in reversed(flips):
        high = (place & flip) != 0
        other = hop(value, "replica", replicas, flip)
        value = jnp.where(
            high, jnp.concatenate([other, value], 1), jnp.concatenate([value, other], 1)
        )
    other = hop(value, "replica", replicas, 1)
    whole = jnp.where(
        core == 1, jnp.concatenate([other, value], 0), jnp.concatenate([value, other], 0)
    )
    return whole.astype(F32)


def body(
    shards,
    replicas,
    tokens,
    cond,
    cot,
    w_mod,
    b_mod,
    w_qkv,
    b_qv,
    w_out,
    b_out,
    w_fc1,
    b_fc1,
    w_fc2,
    b_fc2,
):
    place = lax.axis_index("shard")
    core = lax.axis_index("replica") & 1
    row_count, width = tokens.shape
    head_count = width // 64
    mod_rows = w_mod.shape[0]

    cond_f = cond.astype(F32)
    cond_act = jax.nn.silu(cond_f).astype(BF16)
    biases = [b_qv, b_out, b_fc1, b_fc2]
    note = jnp.concatenate([cond_act[0]] + biases)[None]
    notes = jnp.concatenate(
        [note] + [hop(note, "shard", shards, number) for number in range(1, shards)], 0
    )
    group_act = notes[:, :width]
    group_cols = lax.dynamic_slice_in_dim(group_act, place * mod_rows, mod_rows, 1)
    bias_rows = xor_rows(notes[:, width:].astype(F32), place)
    full_bias = []
    start = 0
    for piece in biases:
        full_bias.append(bias_rows[:, start : start + piece.shape[0]].reshape(-1))
        start += piece.shape[0]
    bias_qv, bias_out, bias_fc1, bias_fc2 = full_bias

    partial = matmul(group_cols, w_mod)
    own_bias = lax.dynamic_update_slice(
        jnp.zeros((6 * width,), F32), b_mod.astype(F32), (place * b_mod.shape[0],)
    )
    partial = partial + own_bias
    modulation = partial[0:1]
    for number in range(1, shards):
        modulation = modulation + hop(partial[number : number + 1], "shard", shards, number)
    shift_a, scale_a, gate_a, shift_b, scale_b, gate_b = [
        modulation[:, at * width : (at + 1) * width] for at in range(6)
    ]

    mine_qkv, _ = gather_weight(w_qkv, core, shards)
    mine_out, _ = gather_weight(w_out, core, shards)
    mine_fc1, _ = gather_weight(w_fc1, core, shards)
    mine_fc2, _ = gather_weight(w_fc2, core, shards)
    full_qkv = join_weight(w_qkv, mine_qkv, replicas, shards)
    full_out = join_weight(w_out, mine_out, replicas, shards)
    full_fc1 = join_weight(w_fc1, mine_fc1, replicas, shards)
    full_fc2 = join_weight(w_fc2, mine_fc2, replicas, shards)

    def to_local(values):
        block = values.shape[1] // shards
        half = block // 2
        cols = [lax.dynamic_slice_in_dim(values, place * block, block, 1)]
        for number in range(1, shards):
            for side in (core, 1 - core):
                cols.append(
                    lax.dynamic_slice_in_dim(
                        values, (place ^ number) * block + side * half, half, 1
                    )
                )
        return jnp.concatenate(cols, 1)

    def from_local(values):
        block = values.shape[1] // shards
        half = block // 2
        cols = []
        for at in range(shards):
            number = place ^ at
            for side in range(2):
                there = jnp.where(number == 0, side, side ^ core)
                cols.append(
                    lax.dynamic_slice_in_dim(values, number * block + there * half, half, 1)
                )
        return jnp.concatenate(cols, 1)

    inputs = tokens.astype(F32)
    norm_a, rstd_a = layer_norm(inputs)
    modul_a = to_local((norm_a * (1.0 + scale_a) + shift_a).astype(BF16))
    projected = matmul(modul_a, full_qkv)
    head_shape = (row_count, head_count, 64)
    queries = (projected[:, :width] + bias_qv[:width]).astype(BF16).reshape(head_shape)
    keys_b = projected[:, width : 2 * width].astype(BF16).reshape(head_shape)
    values_b = (projected[:, 2 * width :] + bias_qv[width:]).astype(BF16).reshape(head_shape)
    scores = batched("qhd,khd->hqk", queries, keys_b) * 0.125
    row_max = jnp.max(scores, -1, keepdims=True)
    exp_scores = jnp.exp(scores - row_max)
    row_total = jnp.sum(exp_scores, -1, keepdims=True)
    probs_f = exp_scores / row_total
    attn_probs = probs_f.astype(BF16)
    attended = batched("hqk,khd->qhd", attn_probs, values_b).astype(BF16)
    attn_flat = to_local(attended.reshape(row_count, width))
    branch_a = matmul(attn_flat, full_out) + bias_out
    middle = inputs + gate_a * branch_a
    norm_b, rstd_b = layer_norm(middle)
    modul_b = to_local((norm_b * (1.0 + scale_b) + shift_b).astype(BF16))
    hidden_pre = matmul(modul_b, full_fc1) + bias_fc1
    hidden = to_local(gelu_tanh(hidden_pre).astype(BF16))
    grad_out = cot.astype(F32)
    grad_branch_b = grad_out * gate_b
    branch_b_low = grad_branch_b.astype(BF16)
    total_fc2 = reduce_grad(matmul_tn(hidden, branch_b_low), core, shards, replicas)
    branch_b = matmul(hidden, full_fc2) + bias_fc2
    output = (middle + gate_b * branch_b).astype(BF16)
    grad_gate_b = jnp.sum(grad_out * branch_b, 0)
    grad_b_fc2 = jnp.sum(grad_branch_b, 0)
    grad_hidden = from_local(matmul_nt(branch_b_low, full_fc2))
    _, gelu_back = jax.vjp(gelu_tanh, hidden_pre)
    grad_pre = gelu_back(grad_hidden)[0]
    grad_pre_low = grad_pre.astype(BF16)
    total_fc1 = reduce_grad(matmul_tn(modul_b, grad_pre_low), core, shards, replicas)
    grad_b_fc1 = jnp.sum(grad_pre, 0)
    grad_modul_b = from_local(matmul_nt(grad_pre_low, full_fc1))
    grad_shift_b = jnp.sum(grad_modul_b, 0)
    grad_scale_b = jnp.sum(grad_modul_b * norm_b, 0)
    grad_middle = grad_out + norm_back(grad_modul_b * (1.0 + scale_b), norm_b, rstd_b)
    grad_gate_a = jnp.sum(grad_middle * branch_a, 0)
    grad_branch_a = grad_middle * gate_a
    branch_a_low = grad_branch_a.astype(BF16)
    total_out = reduce_grad(matmul_tn(attn_flat, branch_a_low), core, shards, replicas)
    grad_b_out = jnp.sum(grad_branch_a, 0)
    grad_attended = from_local(matmul_nt(branch_a_low, full_out)).astype(BF16).reshape(head_shape)
    grad_values = batched("hqk,qhd->khd", attn_probs, grad_attended)
    grad_probs = batched("qhd,khd->hqk", grad_attended, values_b)
    delta_rows = jnp.sum(grad_attended.astype(F32) * attended.astype(F32), -1)
    grad_scores = (probs_f * (grad_probs - delta_rows.T[..., None]) * 0.125).astype(BF16)
    grad_queries = batched("hqk,khd->qhd", grad_scores, keys_b)
    grad_keys = batched("hqk,qhd->khd", grad_scores, queries)
    grad_proj = jnp.concatenate(
        [
            grad_queries.reshape(row_count, width),
            grad_keys.reshape(row_count, width),
            grad_values.reshape(row_count, width),
        ],
        1,
    )
    grad_proj_low = grad_proj.astype(BF16)
    total_qkv = reduce_grad(matmul_tn(modul_a, grad_proj_low), core, shards, replicas)
    grad_b_qv = jnp.concatenate(
        [jnp.sum(grad_proj[:, :width], 0), jnp.sum(grad_proj[:, 2 * width :], 0)]
    )
    grad_modul_a = from_local(matmul_nt(grad_proj_low, full_qkv))
    grad_shift_a = jnp.sum(grad_modul_a, 0)
    grad_scale_a = jnp.sum(grad_modul_a * norm_a, 0)
    grad_inputs = grad_middle + norm_back(grad_modul_a * (1.0 + scale_a), norm_a, rstd_a)
    grad_modulation = jnp.concatenate(
        [grad_shift_a, grad_scale_a, grad_gate_a, grad_shift_b, grad_scale_b, grad_gate_b]
    )

    bias_grads = [grad_b_qv, grad_b_out, grad_b_fc1, grad_b_fc2]
    owned = jnp.concatenate([piece.reshape(shards, -1) for piece in bias_grads], 1).astype(BF16)
    own_span = owned.shape[1]
    mod_span = 6 * width
    news = jnp.concatenate([grad_modulation.astype(BF16), owned.reshape(-1)])[None]
    group_news = jnp.concatenate(
        [news] + [hop(news, "shard", shards, number) for number in range(1, shards)], 0
    )
    group_mod = group_news[:, :mod_span]
    own_bias_part = jnp.sum(
        lax.dynamic_slice_in_dim(group_news, mod_span + place * own_span, own_span, 1).astype(F32),
        0,
    )
    back_rows = matmul_nt(group_mod, w_mod)
    came_rows = [back_rows[0:1]]
    for number in range(1, shards):
        came_rows.append(hop(back_rows[number : number + 1], "shard", shards, number))
    grad_cond_act = xor_rows(jnp.concatenate(came_rows, 0), place).reshape(1, width)
    _, silu_back = jax.vjp(jax.nn.silu, cond_f)
    grad_cond = silu_back(grad_cond_act)[0]

    share = jnp.concatenate(
        [
            jnp.concatenate([group_mod, group_cols], 1).reshape(1, -1),
            own_bias_part.astype(BF16)[None],
        ],
        1,
    )
    flip = 1
    while flip < replicas:
        share = jnp.concatenate([share, hop(share, "replica", replicas, flip)], 0)
        flip *= 2
    mod_part = share[:, : shards * (mod_span + mod_rows)].reshape(-1, mod_span + mod_rows)
    all_mod = mod_part[:, :mod_span]
    all_cols = mod_part[:, mod_span:]
    total_mod = matmul_tn(all_cols, all_mod)
    own_mod = lax.dynamic_slice_in_dim(all_mod, place * b_mod.shape[0], b_mod.shape[0], 1)
    total_b_mod = jnp.sum(own_mod.astype(F32), 0)
    bias_sum = jnp.sum(share[:, shards * (mod_span + mod_rows) :].astype(F32), 0)
    bias_totals = []
    start = 0
    for piece in biases:
        bias_totals.append(bias_sum[start : start + piece.shape[0]])
        start += piece.shape[0]
    return (
        output,
        grad_inputs,
        grad_cond,
        total_mod,
        total_b_mod,
        total_qkv,
        bias_totals[0],
        total_out,
        bias_totals[1],
        total_fc1,
        bias_totals[2],
        total_fc2,
        bias_totals[3],
    )


def solution(mesh):
    shards = mesh.shape["shard"]
    replicas = mesh.shape["replica"]
    both = P(("shard", "replica"), None)
    weight = P("shard", None)
    bias = P("shard")
    pairs = (weight, bias) * 5

    def run(*args):
        return body(shards, replicas, *args)

    return jax.shard_map(
        run,
        mesh=mesh,
        in_specs=(both, both, both) + pairs,
        out_specs=(both, both, both) + pairs,
        check_vma=False,
    )
```

```python
import functools

import jax
import jax.numpy as jnp
from jax import lax
from jax.experimental import pallas as pl
from jax.experimental.pallas import tpu as pltpu
from jax.sharding import PartitionSpec as P

F32 = jnp.float32
BF16 = jnp.bfloat16
HEAD = 64
CHUNK = 512


def dot_nn(left, right):
    return lax.dot_general(left, right, (((1,), (0,)), ((), ())), preferred_element_type=F32)


def dot_tn(left, right):
    return lax.dot_general(left, right, (((0,), (0,)), ((), ())), preferred_element_type=F32)


def dot_nt(left, right):
    return lax.dot_general(left, right, (((1,), (1,)), ((), ())), preferred_element_type=F32)


def layer_norm(values):
    center = values - jnp.mean(values, -1, keepdims=True)
    rstd_val = lax.rsqrt(jnp.mean(center * center, -1, keepdims=True) + 1e-06)
    return (center * rstd_val, rstd_val)


def norm_back(grad_norm, normed, rstd_val):
    return rstd_val * (
        grad_norm
        - jnp.mean(grad_norm, -1, keepdims=True)
        - normed * jnp.mean(grad_norm * normed, -1, keepdims=True)
    )


def hop(value, axis, size, flip):
    return lax.ppermute(value, axis, [(at, at ^ flip) for at in range(size)])


def bits_of(number):
    return [1 << at for at in range(number.bit_length()) if number >> at & 1]


def by_weight(count):
    return sorted(range(1, count), key=lambda number: (bin(number).count("1"), number))


def xor_rows(rows, place):
    count = rows.shape[0]
    flip = 1
    while flip < count:
        swapped = rows.reshape(count // (2 * flip), 2, flip, -1)[:, ::-1].reshape(rows.shape)
        rows = jnp.where((place & flip) != 0, swapped, rows)
        flip *= 2
    return rows


def piece_layout(shards, width):
    layout = []
    for number in by_weight(shards):
        ways = len(bits_of(number))
        part = width // ways
        layout += [(number, at * part, part) for at in range(ways)]
    return layout


def gather_weight(half, shards, replicas, first):
    width = half.shape[1]
    mine = {0: half}
    pieces = []
    for number in by_weight(shards):
        ways = bits_of(number)
        part = width // len(ways)
        got = []
        for at, flip in enumerate(ways):
            source = mine[number ^ flip]
            if len(ways) > 1:
                source = source[:, at * part : (at + 1) * part]
            got.append(hop(source, "shard", shards, flip))
        mine[number] = got[0] if len(got) == 1 else jnp.concatenate(got, 1)
        pieces += got
        if len(ways) == 1:
            first.append(got[0])
    return pieces + [hop(piece, "replica", replicas, 1) for piece in pieces]


def reduce_grad(keep, send, shards, replicas):
    came = [hop(piece, "replica", replicas, 1) for piece in send]
    parts = [mine.astype(F32) + other.astype(F32) for mine, other in zip(keep, came)]
    width = parts[0].shape[1]
    for number in reversed(by_weight(shards)):
        ways = bits_of(number)
        part = width // len(ways)
        for at, flip in enumerate(ways):
            target = number ^ flip
            if len(ways) == 1:
                sent = parts[number].astype(BF16)
                parts[target] = parts[target] + hop(sent, "shard", shards, flip).astype(F32)
            else:
                low, high = at * part, (at + 1) * part
                sent = parts[number][:, low:high].astype(BF16)
                got = hop(sent, "shard", shards, flip).astype(F32)
                old = parts[target]
                parts[target] = jnp.concatenate(
                    [old[:, :low], old[:, low:high] + got, old[:, high:]], 1
                )
    value = parts[0]
    chips = replicas // 2
    chip = lax.axis_index("replica") // 2
    span = width // chips
    total = lax.dynamic_slice_in_dim(value, chip * span, span, 1)
    for flip in range(1, chips):
        sent = lax.dynamic_slice_in_dim(value, (chip ^ flip) * span, span, 1).astype(BF16)
        total = total + hop(sent, "replica", replicas, 2 * flip).astype(F32)
    total = total.astype(BF16)
    cols = [total] + [hop(total, "replica", replicas, 2 * flip) for flip in range(1, chips)]
    stack = jnp.stack(cols, 0)
    whole = xor_blocks(stack, chip)
    whole = whole.transpose(1, 0, 2).reshape(value.shape)
    other = hop(whole, "replica", replicas, 1)
    core = lax.axis_index("replica") % 2
    both = jnp.where(
        core == 1, jnp.concatenate([other, whole], 0), jnp.concatenate([whole, other], 0)
    )
    return both.astype(F32)


def xor_blocks(stack, place):
    count = stack.shape[0]
    flip = 1
    while flip < count:
        swapped = stack.reshape((count // (2 * flip), 2, flip) + stack.shape[1:])[:, ::-1]
        stack = jnp.where((place & flip) != 0, swapped.reshape(stack.shape), stack)
        flip *= 2
    return stack


def start_fetch(own, pieces, whole, sems, shards):
    place = lax.axis_index("shard")
    core = lax.axis_index("replica") % 2
    total_rows, width = whole.shape
    block = total_rows // shards
    half = block // 2
    copies = []

    def add(source, row, low, cols):
        rows = source.shape[0]
        there = whole.at[pl.ds(pl.multiple_of(row, 16), rows), pl.ds(low, cols)]
        copy = pltpu.make_async_copy(source, there, sems.at[len(copies)])
        copy.start()
        copies.append(copy)

    low = 0
    for part in own:
        cols = part.shape[1]
        add(part, place * block, low, cols)
        low += cols
    layout = piece_layout(shards, width)
    for at, (number, first, cols) in enumerate(layout):
        for side, source in ((core, pieces[at]), (1 - core, pieces[len(layout) + at])):
            add(source, (place ^ number) * block + side * half, first, cols)
    return copies


def fetch_count(shards, own):
    return own + 2 * len(piece_layout(shards, 1 << 20))


def start_emit(grad, keep, send, sems, shards):
    place = lax.axis_index("shard")
    core = lax.axis_index("replica") % 2
    block = grad.shape[0] // shards
    half = block // 2
    copies = []
    for number in range(shards):
        for side, target in ((core, keep[number]), (1 - core, send[number])):
            row = pl.multiple_of((place ^ number) * block + side * half, 16)
            copy = pltpu.make_async_copy(
                grad.at[pl.ds(row, half), :], target, sems.at[len(copies)]
            )
            copy.start()
            copies.append(copy)
    return copies


def wait_all(copies):
    for copy in copies:
        copy.wait()


def mod_piece(mod, at, width):
    return mod[:, at * width : (at + 1) * width]


def take(refs, count):
    head = refs[:count]
    del refs[:count]
    return head


def gelu_parts(pre):
    scale = 0.7978845608028654
    square = pre * pre
    inner = jnp.tanh(scale * (pre + 0.044715 * (square * pre)))
    value = 0.5 * pre * (1.0 + inner)
    slope = 0.5 * (1.0 + inner) + 0.5 * pre * (1.0 - inner * inner) * (
        scale * (1.0 + 0.134145 * square)
    )
    return value, slope


def attend_kernel(shards, *refs):
    refs = list(refs)
    tokens, mod, bias_qv, bias_out = take(refs, 4)
    own = take(refs, 2)
    pieces = take(refs, 2 * len(piece_layout(shards, 1 << 20)))
    modul_a, qkv, attended, lse, branch_a, middle, modul_b = take(refs, 7)
    weight, sems = refs
    rows, width = tokens.shape
    copies = start_fetch(own, pieces, weight, sems, shards)
    inputs = tokens[...].astype(F32)
    norm_a, _ = layer_norm(inputs)
    mod_val = mod[...]
    modul = (norm_a * (1.0 + mod_piece(mod_val, 1, width)) + mod_piece(mod_val, 0, width)).astype(
        BF16
    )
    modul_a[...] = modul
    wait_all(copies)
    for at in range(3):
        projected = dot_nn(modul, weight[:, at * width : (at + 1) * width])
        if at != 1:
            low = 0 if at == 0 else width
            projected = projected + bias_qv[:, low : low + width]
        qkv[:, at * width : (at + 1) * width] = projected.astype(BF16)
    lane = lax.broadcasted_iota(jnp.int32, (rows, 2 * HEAD), 1)

    def pair(at, lse_all):
        col = pl.multiple_of(at * 2 * HEAD, 2 * HEAD)
        query = qkv[:, pl.ds(col, 2 * HEAD)]
        key = qkv[:, pl.ds(width + col, 2 * HEAD)]
        value = qkv[:, pl.ds(2 * width + col, 2 * HEAD)]
        out = jnp.zeros((rows, 2 * HEAD), F32)
        for side in range(2):
            mask = (lane < HEAD) if side == 0 else (lane >= HEAD)
            scores = dot_nt(jnp.where(mask, query, 0), key) * 0.125
            top = jnp.max(scores, -1, keepdims=True)
            exps = jnp.exp(scores - top)
            total = jnp.sum(exps, -1, keepdims=True)
            probs = (exps / total).astype(BF16)
            out = out + dot_nn(probs, jnp.where(mask, value, 0))
            lse_all = jnp.where(lane == 2 * at + side, top + jnp.log(total), lse_all)
        attended[:, pl.ds(col, 2 * HEAD)] = out.astype(BF16)
        return lse_all

    lse[...] = lax.fori_loop(
        0, width // (2 * HEAD), pair, jnp.zeros((rows, 2 * HEAD), F32)
    )
    branch = dot_nn(attended[...], weight[:, 3 * width :]) + bias_out[...]
    branch_a[...] = branch
    mid = inputs + mod_piece(mod_val, 2, width) * branch
    middle[...] = mid
    norm_b, _ = layer_norm(mid)
    modul_b[...] = (
        norm_b * (1.0 + mod_piece(mod_val, 4, width)) + mod_piece(mod_val, 3, width)
    ).astype(BF16)


def hidden_kernel(shards, *refs):
    refs = list(refs)
    modul_b, cot, mod, bias_fc1 = take(refs, 4)
    own = take(refs, 1)
    pieces = take(refs, 2 * len(piece_layout(shards, 1 << 20)))
    hidden, slope = take(refs, 2)
    keep = take(refs, shards)
    send = take(refs, shards)
    weight, grad, sems, out_sems = refs
    rows, width = modul_b.shape
    copies = start_fetch(own, pieces, weight, sems, shards)
    low_branch = (cot[...].astype(F32) * mod_piece(mod[...], 5, width)).astype(BF16)
    modul = modul_b[...]
    wait_all(copies)

    def chunk(at, carry):
        col = pl.multiple_of(at * CHUNK, CHUNK)
        pre = dot_nn(modul, weight[:, pl.ds(col, CHUNK)]) + bias_fc1[:, pl.ds(col, CHUNK)]
        value, rate = gelu_parts(pre)
        value = value.astype(BF16)
        hidden[:, pl.ds(col, CHUNK)] = value
        slope[:, pl.ds(col, CHUNK)] = rate
        grad[pl.ds(col, CHUNK), :] = dot_tn(value, low_branch).astype(BF16)
        return carry

    lax.fori_loop(0, weight.shape[1] // CHUNK, chunk, 0)
    wait_all(start_emit(grad, keep, send, out_sems, shards))


def pre_kernel(shards, *refs):
    refs = list(refs)
    modul_b, cot, mod, slope = take(refs, 4)
    own = take(refs, 1)
    pieces = take(refs, 2 * len(piece_layout(shards, 1 << 20)))
    low_pre, sum_pre = take(refs, 2)
    keep = take(refs, shards)
    send = take(refs, shards)
    weight, grad, turned, sems, out_sems = refs
    rows, width = modul_b.shape
    copies = start_fetch(own, pieces, weight, sems, shards)
    low_branch = (cot[...].astype(F32) * mod_piece(mod[...], 5, width)).astype(BF16)
    turned[...] = modul_b[...].T
    wait_all(copies)

    def chunk(at, carry):
        col = pl.multiple_of(at * CHUNK, CHUNK)
        grad_pre = dot_nt(low_branch, weight[pl.ds(col, CHUNK), :]) * slope[:, pl.ds(col, CHUNK)]
        sum_pre[:, pl.ds(col, CHUNK)] = jnp.sum(grad_pre, 0, keepdims=True)
        low = grad_pre.astype(BF16)
        low_pre[:, pl.ds(col, CHUNK)] = low
        grad[:, pl.ds(col, CHUNK)] = dot_nn(turned[...], low).astype(BF16)
        return carry

    lax.fori_loop(0, weight.shape[0] // CHUNK, chunk, 0)
    wait_all(start_emit(grad, keep, send, out_sems, shards))


def back_kernel(shards, *refs):
    refs = list(refs)
    low_pre, cot, mod, middle, branch_a, modul_a, qkv, attended, lse = take(refs, 9)
    own_fc1 = take(refs, 1)
    pieces_fc1 = take(refs, 2 * len(piece_layout(shards, 1 << 20)))
    own_qkvo = take(refs, 2)
    pieces_qkvo = take(refs, 2 * len(piece_layout(shards, 1 << 20)))
    grad_middle, low_proj, sum_proj, sum_out, grad_mods = take(refs, 5)
    keep = take(refs, shards)
    send = take(refs, shards)
    w_fc1, w_qkvo, grad, grad_att, turned, sems_fc1, sems_qkvo, out_sems = refs
    rows, width = middle.shape
    copies_fc1 = start_fetch(own_fc1, pieces_fc1, w_fc1, sems_fc1, shards)
    copies_qkvo = start_fetch(own_qkvo, pieces_qkvo, w_qkvo, sems_qkvo, shards)
    mod_val = mod[...]
    norm_b, rstd_b = layer_norm(middle[...])
    wait_all(copies_fc1)
    grad_modul = dot_nt(low_pre[...], w_fc1[...])
    grad_mods[0:1, :] = jnp.sum(grad_modul, 0, keepdims=True)
    grad_mods[1:2, :] = jnp.sum(grad_modul * norm_b, 0, keepdims=True)
    grad_mid = cot[...].astype(F32) + norm_back(
        grad_modul * (1.0 + mod_piece(mod_val, 4, width)), norm_b, rstd_b
    )
    grad_middle[...] = grad_mid
    grad_mods[2:3, :] = jnp.sum(grad_mid * branch_a[...], 0, keepdims=True)
    grad_branch = grad_mid * mod_piece(mod_val, 2, width)
    sum_out[...] = jnp.sum(grad_branch, 0, keepdims=True)
    low_branch = grad_branch.astype(BF16)
    wait_all(copies_qkvo)
    grad_att[...] = dot_nt(low_branch, w_qkvo[:, 3 * width :]).astype(BF16)
    turned[...] = attended[...].T
    grad[:, 3 * width :] = dot_nn(turned[...], low_branch).astype(BF16)
    turned[...] = modul_a[...].T
    lane = lax.broadcasted_iota(jnp.int32, (rows, 2 * HEAD), 1)
    lse_val = lse[...]

    def pair(at, carry):
        col = pl.multiple_of(at * 2 * HEAD, 2 * HEAD)
        query = qkv[:, pl.ds(col, 2 * HEAD)]
        key = qkv[:, pl.ds(width + col, 2 * HEAD)]
        value = qkv[:, pl.ds(2 * width + col, 2 * HEAD)]
        grad_out = grad_att[:, pl.ds(col, 2 * HEAD)]
        product = grad_out.astype(F32) * attended[:, pl.ds(col, 2 * HEAD)].astype(F32)
        grad_q = jnp.zeros((rows, 2 * HEAD), F32)
        grad_k = jnp.zeros((rows, 2 * HEAD), F32)
        grad_v = jnp.zeros((rows, 2 * HEAD), F32)
        for side in range(2):
            mask = (lane < HEAD) if side == 0 else (lane >= HEAD)
            query_m = jnp.where(mask, query, 0)
            grad_m = jnp.where(mask, grad_out, 0)
            scores = dot_nt(query_m, key) * 0.125
            log_total = jnp.sum(
                jnp.where(lane == 2 * at + side, lse_val, 0.0), -1, keepdims=True
            )
            probs = jnp.exp(scores - log_total)
            delta = jnp.sum(jnp.where(mask, product, 0.0), -1, keepdims=True)
            grad_scores = (probs * (dot_nt(grad_m, value) - delta) * 0.125).astype(BF16)
            grad_v = grad_v + dot_tn(probs.astype(BF16), grad_m)
            grad_q = grad_q + dot_nn(grad_scores, jnp.where(mask, key, 0))
            grad_k = grad_k + dot_tn(grad_scores, query_m)
        for part, piece in enumerate((grad_q, grad_k, grad_v)):
            there = pl.multiple_of(part * width + col, 2 * HEAD)
            sum_proj[:, pl.ds(there, 2 * HEAD)] = jnp.sum(piece, 0, keepdims=True)
            low = piece.astype(BF16)
            low_proj[:, pl.ds(there, 2 * HEAD)] = low
        return carry

    lax.fori_loop(0, width // (2 * HEAD), pair, 0)

    def chunk(at, carry):
        col = pl.multiple_of(at * width, width)
        grad[:, pl.ds(col, width)] = dot_nn(turned[...], low_proj[:, pl.ds(col, width)]).astype(
            BF16
        )
        return carry

    lax.fori_loop(0, 3, chunk, 0)
    wait_all(start_emit(grad, keep, send, out_sems, shards))


def last_kernel(shards, *refs):
    refs = list(refs)
    low_proj, tokens, mod, grad_middle, hidden, middle, cot, bias_fc2 = take(refs, 8)
    own_qkvo = take(refs, 2)
    pieces_qkvo = take(refs, 2 * len(piece_layout(shards, 1 << 20)))
    own_fc2 = take(refs, 1)
    pieces_fc2 = take(refs, 2 * len(piece_layout(shards, 1 << 20)))
    grad_tokens, mixed, sum_fc2, grad_mods = take(refs, 4)
    w_qkvo, w_fc2, sems_qkvo, sems_fc2 = refs
    rows, width = tokens.shape
    copies_qkvo = start_fetch(own_qkvo, pieces_qkvo, w_qkvo, sems_qkvo, shards)
    copies_fc2 = start_fetch(own_fc2, pieces_fc2, w_fc2, sems_fc2, shards)
    mod_val = mod[...]
    norm_a, rstd_a = layer_norm(tokens[...].astype(F32))
    wait_all(copies_qkvo)
    grad_modul = dot_nt(low_proj[...], w_qkvo[:, : 3 * width])
    grad_mods[0:1, :] = jnp.sum(grad_modul, 0, keepdims=True)
    grad_mods[1:2, :] = jnp.sum(grad_modul * norm_a, 0, keepdims=True)
    grad_tokens[...] = grad_middle[...] + norm_back(
        grad_modul * (1.0 + mod_piece(mod_val, 1, width)), norm_a, rstd_a
    )
    wait_all(copies_fc2)
    branch_b = dot_nn(hidden[...], w_fc2[...]) + bias_fc2[...]
    gate_b = mod_piece(mod_val, 5, width)
    grad_out = cot[...].astype(F32)
    mixed[...] = (middle[...] + gate_b * branch_b).astype(BF16)
    grad_mods[2:3, :] = jnp.sum(grad_out * branch_b, 0, keepdims=True)
    sum_fc2[...] = jnp.sum(grad_out * gate_b, 0, keepdims=True)


def call(kernel, shards, inside, outside, outs, outside_outs, scratch, flops):
    vmem = pl.BlockSpec(memory_space=pltpu.VMEM)
    anywhere = pl.BlockSpec(memory_space=pl.ANY)
    moved = sum(value.size * value.dtype.itemsize for value in inside + outside)
    moved += sum(value.size * value.dtype.itemsize for value in outs + outside_outs)
    return pl.pallas_call(
        functools.partial(kernel, shards),
        out_shape=outs + outside_outs,
        in_specs=[vmem] * len(inside) + [anywhere] * len(outside),
        out_specs=[vmem] * len(outs) + [anywhere] * len(outside_outs),
        scratch_shapes=scratch,
        cost_estimate=pl.CostEstimate(flops=flops, bytes_accessed=moved, transcendentals=0),
        compiler_params=pltpu.CompilerParams(vmem_limit_bytes=56 << 20),
    )(*inside, *outside)


def shape(dims, dtype):
    return jax.ShapeDtypeStruct(dims, dtype)


def body(
    shards,
    replicas,
    tokens,
    cond,
    cot,
    w_mod,
    b_mod,
    w_qkv,
    b_qv,
    w_out,
    b_out,
    w_fc1,
    b_fc1,
    w_fc2,
    b_fc2,
):
    place = lax.axis_index("shard")
    core = lax.axis_index("replica") % 2
    rows, width = tokens.shape
    mod_rows = w_mod.shape[0]
    inner = w_fc1.shape[1]

    cond_f = cond.astype(F32)
    cond_act = jax.nn.silu(cond_f).astype(BF16)
    biases = [b_qv, b_out, b_fc1, b_fc2]
    note = jnp.concatenate([cond_act[0]] + biases)[None]
    notes = jnp.concatenate(
        [note] + [hop(note, "shard", shards, number) for number in range(1, shards)], 0
    )
    group_cols = lax.dynamic_slice_in_dim(notes[:, :width], place * mod_rows, mod_rows, 1)
    bias_rows = xor_rows(notes[:, width:].astype(F32), place)
    full_bias = []
    start = 0
    for piece in biases:
        full_bias.append(bias_rows[:, start : start + piece.shape[0]].reshape(1, -1))
        start += piece.shape[0]
    bias_qv, bias_out, bias_fc1, bias_fc2 = full_bias

    partial = dot_nn(group_cols, w_mod)
    own_bias = lax.dynamic_update_slice(
        jnp.zeros((6 * width,), F32), b_mod.astype(F32), (place * b_mod.shape[0],)
    )
    partial = partial + own_bias
    mod = partial[0:1]
    for number in range(1, shards):
        mod = mod + hop(partial[number : number + 1], "shard", shards, number)

    def halved(weight):
        half = weight.shape[0] // 2
        return lax.dynamic_slice_in_dim(weight, core * half, half, 0)

    first = []
    half_qkvo = jnp.concatenate([halved(w_qkv), halved(w_out)], 1)
    pieces_qkvo = gather_weight(half_qkvo, shards, replicas, first)
    tied = lax.optimization_barrier((w_fc1, *first))
    first = []
    pieces_fc1 = gather_weight(halved(tied[0]), shards, replicas, first)
    tied = lax.optimization_barrier((w_fc2, *first))
    pieces_fc2 = gather_weight(halved(tied[0]), shards, replicas, [])

    pieces = len(piece_layout(shards, 1 << 20)) * 2
    sems = pltpu.SemaphoreType.DMA
    qkvo_scratch = [pltpu.VMEM((width, 4 * width), BF16)]
    fc1_scratch = [pltpu.VMEM((width, inner), BF16)]
    fc2_scratch = [pltpu.VMEM((inner, width), BF16)]
    out_sems = [sems((2 * shards,))]
    half = mod_rows // 2
    half_inner = w_fc2.shape[0] // 2

    modul_a, qkv, attended, lse, branch_a, middle, modul_b = call(
        attend_kernel,
        shards,
        [tokens, mod, bias_qv, bias_out],
        [w_qkv, w_out] + pieces_qkvo,
        [
            shape((rows, width), BF16),
            shape((rows, 3 * width), BF16),
            shape((rows, width), BF16),
            shape((rows, 2 * HEAD), F32),
            shape((rows, width), F32),
            shape((rows, width), F32),
            shape((rows, width), BF16),
        ],
        [],
        qkvo_scratch + [sems((pieces + 2,))],
        10**10,
    )
    hidden, slope, *parts = call(
        hidden_kernel,
        shards,
        [modul_b, cot, mod, bias_fc1],
        [w_fc1] + pieces_fc1,
        [shape((rows, inner), BF16), shape((rows, inner), F32)],
        [shape((half_inner, width), BF16)] * (2 * shards),
        fc1_scratch + fc2_scratch + [sems((pieces + 1,))] + out_sems,
        10**10,
    )
    total_fc2 = reduce_grad(parts[:shards], parts[shards:], shards, replicas)
    low_pre, sum_pre, *parts = call(
        pre_kernel,
        shards,
        [modul_b, cot, mod, slope],
        [w_fc2] + pieces_fc2,
        [shape((rows, inner), BF16), shape((1, inner), F32)],
        [shape((half, inner), BF16)] * (2 * shards),
        fc2_scratch + fc1_scratch + [pltpu.VMEM((width, rows), BF16), sems((pieces + 1,))]
        + out_sems,
        10**10,
    )
    total_fc1 = reduce_grad(parts[:shards], parts[shards:], shards, replicas)
    grad_middle, low_proj, sum_proj, sum_out, mods_b, *parts = call(
        back_kernel,
        shards,
        [low_pre, cot, mod, middle, branch_a, modul_a, qkv, attended, lse],
        [w_fc1] + pieces_fc1 + [w_qkv, w_out] + pieces_qkvo,
        [
            shape((rows, width), F32),
            shape((rows, 3 * width), BF16),
            shape((1, 3 * width), F32),
            shape((1, width), F32),
            shape((3, width), F32),
        ],
        [shape((half, 4 * width), BF16)] * (2 * shards),
        fc1_scratch
        + qkvo_scratch
        + qkvo_scratch
        + [pltpu.VMEM((rows, width), BF16), pltpu.VMEM((width, rows), BF16)]
        + [sems((pieces + 1,)), sems((pieces + 2,))]
        + out_sems,
        10**10,
    )
    total_qkvo = reduce_grad(parts[:shards], parts[shards:], shards, replicas)
    grad_tokens, mixed, sum_fc2, mods_a = call(
        last_kernel,
        shards,
        [low_proj, tokens, mod, grad_middle, hidden, middle, cot, bias_fc2],
        [w_qkv, w_out] + pieces_qkvo + [w_fc2] + pieces_fc2,
        [
            shape((rows, width), F32),
            shape((rows, width), BF16),
            shape((1, width), F32),
            shape((3, width), F32),
        ],
        [],
        qkvo_scratch + fc2_scratch + [sems((pieces + 2,)), sems((pieces + 1,))],
        10**10,
    )
    grad_modulation = jnp.concatenate(
        [mods_a[0], mods_a[1], mods_b[2], mods_b[0], mods_b[1], mods_a[2]]
    )

    bias_grads = [
        jnp.concatenate([sum_proj[0, :width], sum_proj[0, 2 * width :]]),
        sum_out[0],
        sum_pre[0],
        sum_fc2[0],
    ]
    owned = jnp.concatenate([piece.reshape(shards, -1) for piece in bias_grads], 1).astype(BF16)
    own_span = owned.shape[1]
    mod_span = 6 * width
    news = jnp.concatenate([grad_modulation.astype(BF16), owned.reshape(-1)])[None]
    group_news = jnp.concatenate(
        [news] + [hop(news, "shard", shards, number) for number in range(1, shards)], 0
    )
    group_mod = group_news[:, :mod_span]
    own_bias_part = jnp.sum(
        lax.dynamic_slice_in_dim(group_news, mod_span + place * own_span, own_span, 1).astype(F32),
        0,
    )
    back_rows = dot_nt(group_mod, w_mod)
    came_rows = [back_rows[0:1]]
    for number in range(1, shards):
        came_rows.append(hop(back_rows[number : number + 1], "shard", shards, number))
    grad_cond_act = xor_rows(jnp.concatenate(came_rows, 0), place).reshape(1, width)
    _, silu_back = jax.vjp(jax.nn.silu, cond_f)
    grad_cond = silu_back(grad_cond_act)[0]

    share = jnp.concatenate(
        [
            jnp.concatenate([group_mod, group_cols], 1).reshape(1, -1),
            own_bias_part.astype(BF16)[None],
        ],
        1,
    )
    flip = 1
    while flip < replicas:
        share = jnp.concatenate([share, hop(share, "replica", replicas, flip)], 0)
        flip *= 2
    mod_part = share[:, : shards * (mod_span + mod_rows)].reshape(-1, mod_span + mod_rows)
    all_mod = mod_part[:, :mod_span]
    all_cols = mod_part[:, mod_span:]
    total_mod = dot_tn(all_cols, all_mod)
    own_mod = lax.dynamic_slice_in_dim(all_mod, place * b_mod.shape[0], b_mod.shape[0], 1)
    total_b_mod = jnp.sum(own_mod.astype(F32), 0)
    bias_sum = jnp.sum(share[:, shards * (mod_span + mod_rows) :].astype(F32), 0)
    bias_totals = []
    start = 0
    for piece in biases:
        bias_totals.append(bias_sum[start : start + piece.shape[0]])
        start += piece.shape[0]
    return (
        mixed,
        grad_tokens,
        grad_cond,
        total_mod,
        total_b_mod,
        total_qkvo[:, : 3 * width],
        bias_totals[0],
        total_qkvo[:, 3 * width :],
        bias_totals[1],
        total_fc1,
        bias_totals[2],
        total_fc2,
        bias_totals[3],
    )


def solution(mesh):
    shards = mesh.shape["shard"]
    replicas = mesh.shape["replica"]
    both = P(("shard", "replica"), None)
    pairs = (P("shard", None), P("shard")) * 5

    def run(*args):
        return body(shards, replicas, *args)

    return jax.shard_map(
        run,
        mesh=mesh,
        in_specs=(both, both, both) + pairs,
        out_specs=(both, both, both) + pairs,
        check_vma=False,
    )
```

```python
import functools

import jax
import jax.numpy as jnp
from jax import lax
from jax.experimental import pallas as pl
from jax.experimental.pallas import tpu as pltpu
from jax.sharding import PartitionSpec as P

F32 = jnp.float32
BF16 = jnp.bfloat16
HEAD = 64


def dot_nn(left, right):
    return lax.dot_general(left, right, (((1,), (0,)), ((), ())), preferred_element_type=F32)


def dot_tn(left, right):
    return lax.dot_general(left, right, (((0,), (0,)), ((), ())), preferred_element_type=F32)


def dot_nt(left, right):
    return lax.dot_general(left, right, (((1,), (1,)), ((), ())), preferred_element_type=F32)


def layer_norm(values):
    center = values - jnp.mean(values, -1, keepdims=True)
    rstd_val = lax.rsqrt(jnp.mean(center * center, -1, keepdims=True) + 1e-06)
    return (center * rstd_val, rstd_val)


def norm_back(grad_norm, normed, rstd_val):
    return rstd_val * (
        grad_norm
        - jnp.mean(grad_norm, -1, keepdims=True)
        - normed * jnp.mean(grad_norm * normed, -1, keepdims=True)
    )


def hop(value, axis, size, flip):
    return lax.ppermute(value, axis, [(at, at ^ flip) for at in range(size)])


def bits_of(number):
    return [1 << at for at in range(number.bit_length()) if number >> at & 1]


def by_weight(count):
    return sorted(range(1, count), key=lambda number: (bin(number).count("1"), number))


def xor_rows(rows, place):
    count = rows.shape[0]
    flip = 1
    while flip < count:
        swapped = rows.reshape(count // (2 * flip), 2, flip, -1)[:, ::-1].reshape(rows.shape)
        rows = jnp.where((place & flip) != 0, swapped, rows)
        flip *= 2
    return rows


def part_count(shards):
    return max(1, shards.bit_length() - 1)


def piece_layout(shards, width):
    layout = []
    for number in by_weight(shards):
        parts = 1 if len(bits_of(number)) == 1 else part_count(shards)
        span = width // parts
        layout += [(number, at * span, span) for at in range(parts)]
    return layout


def way(number, at):
    ways = bits_of(number)
    return ways[at % len(ways)]


def after(value, *others):
    return lax.optimization_barrier((value,) + others)[0]


def gate(values, *others):
    return list(lax.optimization_barrier(tuple(values) + others)[: len(values)])


class Gather:
    def __init__(self, half, shards, replicas):
        self.shards, self.replicas = shards, replicas
        self.half = half
        self.parts = part_count(shards)
        self.held = {}
        self.depths = shards.bit_length() - 1

    def operands(self, depth):
        span = self.half.shape[1] // self.parts
        if depth == 1:
            return [self.half]
        found = []
        for number in range(1, self.shards):
            if len(bits_of(number)) == depth:
                for at in range(self.parts):
                    source = self.held[number ^ way(number, at)]
                    if isinstance(source, list):
                        found.append(source[at])
                    else:
                        found.append(source[:, at * span : (at + 1) * span])
        return found

    def send(self, depth, operands):
        got = []
        operands = list(operands)
        for number in range(1, self.shards):
            if len(bits_of(number)) == depth:
                if depth == 1:
                    got.append(hop(operands[0], "shard", self.shards, number))
                else:
                    for at in range(self.parts):
                        flip = way(number, at)
                        got.append(hop(operands.pop(0), "shard", self.shards, flip))
        return got

    def hold(self, depth, got):
        got = list(got)
        for number in range(1, self.shards):
            if len(bits_of(number)) == depth:
                if depth == 1:
                    self.held[number] = got.pop(0)
                else:
                    self.held[number] = [got.pop(0) for _ in range(self.parts)]

    def pieces(self):
        flat = []
        for number in by_weight(self.shards):
            piece = self.held[number]
            flat += piece if isinstance(piece, list) else [piece]
        return flat + [hop(piece, "replica", self.replicas, 1) for piece in flat]


class Reduction:
    def __init__(self, keep, send, shards, replicas, chunks):
        self.keep, self.partner = keep, send
        self.shards, self.replicas, self.chunks = shards, replicas, chunks
        self.parts = part_count(shards)
        self.bits = [1 << at for at in range(shards.bit_length() - 1)]
        self.terms = {at: [] for at in range(self.parts)}

    def swap(self):
        self.came = hop(self.partner, "replica", self.replicas, 1)
        return self.came

    def order(self, at):
        return self.bits[at:] + self.bits[:at]

    def total(self, at, stage):
        order = self.order(at)
        span = self.keep.shape[2] // self.parts
        index = [slice(None)] * len(order)
        for bit in order[:stage]:
            index[len(order) - bit.bit_length()] = slice(0, 1)
        if stage < len(order):
            index[len(order) - order[stage].bit_length()] = slice(1, 2)
        index = tuple(index)
        value = None
        for array in (self.keep, self.came):
            cube = array.reshape((2,) * len(order) + array.shape[1:])
            cube = cube[index + (slice(None), slice(at * span, (at + 1) * span))].astype(F32)
            value = cube if value is None else value + cube
        for term in self.terms[at]:
            value = value + term[index].astype(F32)
        return value

    def ready(self, stage):
        self.sent = [self.total(at, stage).astype(BF16) for at in range(self.parts)]
        return self.sent

    def send(self, stage):
        self.flying = []
        for at in range(self.parts):
            piece = self.sent[at]
            got = hop(
                piece.reshape((-1,) + piece.shape[-2:]), "shard", self.shards, self.order(at)[stage]
            )
            self.flying.append(got.reshape(piece.shape))
        return self.flying

    def land(self, got):
        for at in range(self.parts):
            self.terms[at].append(got[at])

    def own(self):
        values = [self.total(at, len(self.bits)) for at in range(self.parts)]
        values = [value.reshape(value.shape[-2:]) for value in values]
        if self.chunks == 1:
            values = [jnp.concatenate(values, 1)]
        self.values = [value.astype(BF16) for value in values]
        return self.values

    def rounds(self):
        return self.replicas // 2 - 1

    def fold(self, at):
        chips = self.replicas // 2
        mid = chips // 2 - 1
        if at < mid:
            links = [(at, at + 1), (chips - 1 - at, chips - 2 - at)]
        elif at == mid:
            links = [(mid, mid + 1), (mid + 1, mid)]
        else:
            out = 2 * mid - at
            links = [(out + 1, out), (chips - 2 - out, chips - 1 - out)]
        pairs = [(2 * low + core, 2 * high + core) for low, high in links for core in range(2)]
        self.flying = [lax.ppermute(value, "replica", pairs) for value in self.values]
        return self.flying

    def folded(self, at, got):
        chips = self.replicas // 2
        mid = chips // 2 - 1
        chip = lax.axis_index("replica") // 2
        if at <= mid:
            self.values = [
                (value.astype(F32) + piece.astype(F32)).astype(BF16)
                for value, piece in zip(self.values, got)
            ]
        else:
            out = 2 * mid - at
            outer = (chip == out) | (chip == chips - 1 - out)
            self.values = [
                jnp.where(outer, piece, value) for value, piece in zip(self.values, got)
            ]
        return self.values

    def finish(self):
        core = lax.axis_index("replica") % 2
        cols = []
        for value in self.values:
            other = hop(value, "replica", self.replicas, 1)
            cols.append(
                jnp.where(
                    core == 1,
                    jnp.concatenate([other, value], 0),
                    jnp.concatenate([value, other], 0),
                )
            )
        whole = cols[0] if len(cols) == 1 else jnp.concatenate(cols, 1)
        return whole.astype(F32)


def together(*groups):
    flat = [value for group in groups for value in group]
    flat = list(lax.optimization_barrier(tuple(flat)))
    found = []
    for group in groups:
        found.append(flat[: len(group)])
        flat = flat[len(group) :]
    return found


def start_fetch(own, pieces, whole, sems, shards):
    place = lax.axis_index("shard")
    core = lax.axis_index("replica") % 2
    total_rows, width = whole.shape
    block = total_rows // shards
    half = block // 2
    copies = []

    def add(source, row, low, cols):
        rows = source.shape[0]
        there = whole.at[pl.ds(pl.multiple_of(row, 16), rows), pl.ds(low, cols)]
        copy = pltpu.make_async_copy(source, there, sems.at[len(copies)])
        copy.start()
        copies.append(copy)

    low = 0
    for part in own:
        cols = part.shape[1]
        add(part, place * block, low, cols)
        low += cols
    layout = piece_layout(shards, width)
    for at, (number, first, cols) in enumerate(layout):
        for side, source in ((core, pieces[at]), (1 - core, pieces[len(layout) + at])):
            add(source, (place ^ number) * block + side * half, first, cols)
    return copies


def start_emit(grad, low, cols, keep, send, sems, shards, copies):
    place = lax.axis_index("shard")
    core = lax.axis_index("replica") % 2
    block = grad.shape[0] // shards
    half = block // 2
    for number in range(shards):
        for side, target in ((core, keep), (1 - core, send)):
            row = pl.multiple_of((place ^ number) * block + side * half, 16)
            copy = pltpu.make_async_copy(
                grad.at[pl.ds(row, half), pl.ds(low, cols)],
                target.at[number, :, pl.ds(low, cols)],
                sems.at[len(copies)],
            )
            copy.start()
            copies.append(copy)


def wait_all(copies):
    for copy in copies:
        copy.wait()


def mod_piece(mod, at, width):
    return mod[:, at * width : (at + 1) * width]


def piece_total(shards):
    return 2 * len(piece_layout(shards, 1 << 20))


def take(refs, count):
    head = refs[:count]
    del refs[:count]
    return head


def gelu_parts(pre):
    scale = 0.7978845608028654
    square = pre * pre
    inner = jnp.tanh(scale * (pre + 0.044715 * (square * pre)))
    value = 0.5 * pre * (1.0 + inner)
    slope = 0.5 * (1.0 + inner) + 0.5 * pre * (1.0 - inner * inner) * (
        scale * (1.0 + 0.134145 * square)
    )
    return value, slope


def attend_kernel(shards, *refs):
    refs = list(refs)
    tokens, mod, bias_qv, bias_out = take(refs, 4)
    own = take(refs, 2)
    pieces = take(refs, piece_total(shards))
    modul_a, qkv, attended, lse, branch_a, middle, modul_b = take(refs, 7)
    weight, sems = refs
    rows, width = tokens.shape
    copies = start_fetch(own, pieces, weight, sems, shards)
    inputs = tokens[...].astype(F32)
    norm_a, _ = layer_norm(inputs)
    mod_val = mod[...]
    modul = (norm_a * (1.0 + mod_piece(mod_val, 1, width)) + mod_piece(mod_val, 0, width)).astype(
        BF16
    )
    modul_a[...] = modul
    wait_all(copies)
    for at in range(3):
        projected = dot_nn(modul, weight[:, at * width : (at + 1) * width])
        if at != 1:
            low = 0 if at == 0 else width
            projected = projected + bias_qv[:, low : low + width]
        qkv[:, at * width : (at + 1) * width] = projected.astype(BF16)
    lane = lax.broadcasted_iota(jnp.int32, (rows, 2 * HEAD), 1)

    def pair(at, lse_all):
        col = pl.multiple_of(at * 2 * HEAD, 2 * HEAD)
        query = qkv[:, pl.ds(col, 2 * HEAD)]
        key = qkv[:, pl.ds(width + col, 2 * HEAD)]
        value = qkv[:, pl.ds(2 * width + col, 2 * HEAD)]
        out = jnp.zeros((rows, 2 * HEAD), F32)
        for side in range(2):
            mask = (lane < HEAD) if side == 0 else (lane >= HEAD)
            scores = dot_nt(jnp.where(mask, query, 0), key) * 0.125
            top = jnp.max(scores, -1, keepdims=True)
            exps = jnp.exp(scores - top)
            total = jnp.sum(exps, -1, keepdims=True)
            probs = (exps / total).astype(BF16)
            out = out + dot_nn(probs, jnp.where(mask, value, 0))
            lse_all = jnp.where(lane == 2 * at + side, top + jnp.log(total), lse_all)
        attended[:, pl.ds(col, 2 * HEAD)] = out.astype(BF16)
        return lse_all

    lse[...] = lax.fori_loop(
        0, width // (2 * HEAD), pair, jnp.zeros((rows, 2 * HEAD), F32)
    )
    branch = dot_nn(attended[...], weight[:, 3 * width :]) + bias_out[...]
    branch_a[...] = branch
    mid = inputs + mod_piece(mod_val, 2, width) * branch
    middle[...] = mid
    norm_b, _ = layer_norm(mid)
    modul_b[...] = (
        norm_b * (1.0 + mod_piece(mod_val, 4, width)) + mod_piece(mod_val, 3, width)
    ).astype(BF16)


def hidden_kernel(shards, *refs):
    refs = list(refs)
    modul_b, cot, mod, bias_fc1 = take(refs, 4)
    own = take(refs, 1)
    pieces = take(refs, piece_total(shards))
    hidden, slope = take(refs, 2)
    keep, send = take(refs, 2)
    weight, grad, sems, out_sems = refs
    rows, width = modul_b.shape
    copies = start_fetch(own, pieces, weight, sems, shards)
    low_branch = (cot[...].astype(F32) * mod_piece(mod[...], 5, width)).astype(BF16)
    modul = modul_b[...]
    wait_all(copies)
    place = lax.axis_index("shard")
    core = lax.axis_index("replica") % 2
    span = weight.shape[1] // shards
    half = span // 2
    outs = []
    for number in range(shards - 1, -1, -1):
        col = pl.multiple_of((place ^ number) * span, 128)
        pre = dot_nn(modul, weight[:, pl.ds(col, span)]) + bias_fc1[:, pl.ds(col, span)]
        value, rate = gelu_parts(pre)
        value = value.astype(BF16)
        hidden[:, pl.ds(col, span)] = value
        slope[:, pl.ds(col, span)] = rate
        grad[number] = dot_tn(value, low_branch).astype(BF16)
        for side, target in ((core, keep), (1 - core, send)):
            row = pl.multiple_of(side * half, 16)
            copy = pltpu.make_async_copy(
                grad.at[number, pl.ds(row, half), :], target.at[number], out_sems.at[len(outs)]
            )
            copy.start()
            outs.append(copy)
    wait_all(outs)


def pre_kernel(shards, *refs):
    refs = list(refs)
    modul_b, cot, mod, slope = take(refs, 4)
    own = take(refs, 1)
    pieces = take(refs, piece_total(shards))
    low_pre, sum_pre = take(refs, 2)
    keep, send = take(refs, 2)
    weight, grad, turned, sems, out_sems = refs
    rows, width = modul_b.shape
    copies = start_fetch(own, pieces, weight, sems, shards)
    low_branch = (cot[...].astype(F32) * mod_piece(mod[...], 5, width)).astype(BF16)
    turned[...] = modul_b[...].T
    wait_all(copies)

    outs = []
    for col in range(0, weight.shape[0], width):
        cols = slice(col, col + width)
        grad_pre = dot_nt(low_branch, weight[cols, :]) * slope[:, cols]
        sum_pre[:, cols] = jnp.sum(grad_pre, 0, keepdims=True)
        low = grad_pre.astype(BF16)
        low_pre[:, cols] = low
        grad[:, cols] = dot_nn(turned[...], low).astype(BF16)
        start_emit(grad, col, width, keep, send, out_sems, shards, outs)
    wait_all(outs)


def middle_kernel(shards, *refs):
    refs = list(refs)
    low_pre, cot, mod, middle, branch_a = take(refs, 5)
    own = take(refs, 1)
    pieces = take(refs, piece_total(shards))
    grad_middle, low_branch_a, sum_out, grad_mods = take(refs, 4)
    weight, sems = refs
    rows, width = middle.shape
    copies = start_fetch(own, pieces, weight, sems, shards)
    mod_val = mod[...]
    norm_b, rstd_b = layer_norm(middle[...])
    wait_all(copies)
    grad_modul = dot_nt(low_pre[...], weight[...])
    grad_mods[0:1, :] = jnp.sum(grad_modul, 0, keepdims=True)
    grad_mods[1:2, :] = jnp.sum(grad_modul * norm_b, 0, keepdims=True)
    grad_mid = cot[...].astype(F32) + norm_back(
        grad_modul * (1.0 + mod_piece(mod_val, 4, width)), norm_b, rstd_b
    )
    grad_middle[...] = grad_mid
    grad_mods[2:3, :] = jnp.sum(grad_mid * branch_a[...], 0, keepdims=True)
    grad_branch = grad_mid * mod_piece(mod_val, 2, width)
    sum_out[...] = jnp.sum(grad_branch, 0, keepdims=True)
    low_branch_a[...] = grad_branch.astype(BF16)


def back_kernel(shards, *refs):
    refs = list(refs)
    low_branch_a, modul_a, qkv, attended, lse = take(refs, 5)
    own = take(refs, 2)
    pieces = take(refs, piece_total(shards))
    low_proj, sum_proj = take(refs, 2)
    keep, send = take(refs, 2)
    weight, grad, grad_att, turned, sems, out_sems = refs
    rows, width = modul_a.shape
    copies = start_fetch(own, pieces, weight, sems, shards)
    low_branch = low_branch_a[...]
    outs = []
    turned[...] = attended[...].T
    grad[:, 3 * width :] = dot_nn(turned[...], low_branch).astype(BF16)
    start_emit(grad, 3 * width, width, keep, send, out_sems, shards, outs)
    turned[...] = modul_a[...].T
    wait_all(copies)
    grad_att[...] = dot_nt(low_branch, weight[:, 3 * width :]).astype(BF16)
    lane = lax.broadcasted_iota(jnp.int32, (rows, 2 * HEAD), 1)
    lse_val = lse[...]

    def pair(at, carry):
        col = pl.multiple_of(at * 2 * HEAD, 2 * HEAD)
        query = qkv[:, pl.ds(col, 2 * HEAD)]
        key = qkv[:, pl.ds(width + col, 2 * HEAD)]
        value = qkv[:, pl.ds(2 * width + col, 2 * HEAD)]
        grad_out = grad_att[:, pl.ds(col, 2 * HEAD)]
        product = grad_out.astype(F32) * attended[:, pl.ds(col, 2 * HEAD)].astype(F32)
        grad_q = jnp.zeros((rows, 2 * HEAD), F32)
        grad_k = jnp.zeros((rows, 2 * HEAD), F32)
        grad_v = jnp.zeros((rows, 2 * HEAD), F32)
        for side in range(2):
            mask = (lane < HEAD) if side == 0 else (lane >= HEAD)
            query_m = jnp.where(mask, query, 0)
            grad_m = jnp.where(mask, grad_out, 0)
            scores = dot_nt(query_m, key) * 0.125
            log_total = jnp.sum(
                jnp.where(lane == 2 * at + side, lse_val, 0.0), -1, keepdims=True
            )
            probs = jnp.exp(scores - log_total)
            delta = jnp.sum(jnp.where(mask, product, 0.0), -1, keepdims=True)
            grad_scores = (probs * (dot_nt(grad_m, value) - delta) * 0.125).astype(BF16)
            grad_v = grad_v + dot_tn(probs.astype(BF16), grad_m)
            grad_q = grad_q + dot_nn(grad_scores, jnp.where(mask, key, 0))
            grad_k = grad_k + dot_tn(grad_scores, query_m)
        for part, piece in enumerate((grad_q, grad_k, grad_v)):
            there = pl.multiple_of(part * width + col, 2 * HEAD)
            sum_proj[:, pl.ds(there, 2 * HEAD)] = jnp.sum(piece, 0, keepdims=True)
            low_proj[:, pl.ds(there, 2 * HEAD)] = piece.astype(BF16)
        return carry

    lax.fori_loop(0, width // (2 * HEAD), pair, 0, unroll=2)
    for at in range(3):
        cols = slice(at * width, (at + 1) * width)
        grad[:, cols] = dot_nn(turned[...], low_proj[:, cols]).astype(BF16)
        start_emit(grad, at * width, width, keep, send, out_sems, shards, outs)
    wait_all(outs)


def last_kernel(shards, *refs):
    refs = list(refs)
    low_proj, tokens, mod, grad_middle, hidden, middle, cot, bias_fc2 = take(refs, 8)
    sum_proj, sum_out, sum_pre, mods_b = take(refs, 4)
    own_qkvo = take(refs, 2)
    pieces_qkvo = take(refs, piece_total(shards))
    own_fc2 = take(refs, 1)
    pieces_fc2 = take(refs, piece_total(shards))
    grad_tokens, mixed, news = take(refs, 3)
    w_qkvo, w_fc2, sems_qkvo, sems_fc2 = refs
    rows, width = tokens.shape
    copies_qkvo = start_fetch(own_qkvo, pieces_qkvo, w_qkvo, sems_qkvo, shards)
    copies_fc2 = start_fetch(own_fc2, pieces_fc2, w_fc2, sems_fc2, shards)
    mod_val = mod[...]
    norm_a, rstd_a = layer_norm(tokens[...].astype(F32))
    wait_all(copies_qkvo)
    grad_modul = dot_nt(low_proj[...], w_qkvo[:, : 3 * width])
    sums = [
        jnp.sum(grad_modul, 0, keepdims=True),
        jnp.sum(grad_modul * norm_a, 0, keepdims=True),
        mods_b[2:3, :],
        mods_b[0:1, :],
        mods_b[1:2, :],
    ]
    grad_tokens[...] = grad_middle[...] + norm_back(
        grad_modul * (1.0 + mod_piece(mod_val, 1, width)), norm_a, rstd_a
    )
    wait_all(copies_fc2)
    branch_b = dot_nn(hidden[...], w_fc2[...]) + bias_fc2[...]
    gate_b = mod_piece(mod_val, 5, width)
    grad_out = cot[...].astype(F32)
    mixed[...] = (middle[...] + gate_b * branch_b).astype(BF16)
    sums.append(jnp.sum(grad_out * branch_b, 0, keepdims=True))
    sums += [sum_proj[:, :width], sum_proj[:, 2 * width :], sum_out[...], sum_pre[...]]
    sums.append(jnp.sum(grad_out * gate_b, 0, keepdims=True))
    low = 0
    for piece in sums:
        news[:, low : low + piece.shape[1]] = piece.astype(BF16)
        low += piece.shape[1]


def share_kernel(shards, *refs):
    refs = list(refs)
    news = take(refs, shards)
    w_mod, group_cols = take(refs, 2)
    back = take(refs, shards)
    share, rows_ref = refs
    span = w_mod.shape[1]
    cols = w_mod.shape[0]
    rows_ref[...] = jnp.zeros_like(rows_ref)
    biases = jnp.zeros((1, news[0].shape[1] - span), F32)
    for at in range(shards):
        rows_ref[at : at + 1, :span] = news[at][:, :span].astype(F32)
        biases = biases + news[at][:, span:].astype(F32)
    low = rows_ref[:, :span].astype(BF16)
    rows_back = dot_nt(low, w_mod[...])
    for at in range(shards):
        for owner in range(shards):
            back[at][:, owner * cols : (owner + 1) * cols] = jnp.where(
                lax.axis_index("shard") == owner, rows_back[at : at + 1, :], 0.0
            )
    rows_ref[:shards, span : span + cols] = group_cols[...].astype(F32)
    part = biases.shape[1] // 2
    for at in range(2):
        rows_ref[shards + at : shards + at + 1, :part] = biases[:, at * part : (at + 1) * part]
    share[0] = rows_ref[...].astype(BF16)


def total_kernel(shards, *refs):
    share, total_mod, own_mod, own_qv, own_out, own_fc1, own_fc2 = refs
    cols, span = total_mod.shape
    groups, count, _ = share.shape
    row = lax.broadcasted_iota(jnp.int32, (count, 1), 0)
    total = jnp.zeros((count, share.shape[2]), F32)
    for at in range(groups):
        total = total + share[at].astype(F32)
    place = lax.axis_index("shard")

    def own(target, values):
        size = target.shape[1]
        found = jnp.zeros((1, size), F32)
        for at in range(shards):
            found = jnp.where(place == at, values[:, at * size : (at + 1) * size], found)
        target[...] = found

    own(own_mod, jnp.sum(jnp.where(row < shards, total[:, :span], 0.0), 0, keepdims=True))
    part = shards * (own_qv.shape[1] + own_out.shape[1] + own_fc1.shape[1] + own_fc2.shape[1]) // 2
    biases = jnp.concatenate(
        [total[shards : shards + 1, :part], total[shards + 1 : shards + 2, :part]], 1
    )
    low = 0
    for target in (own_qv, own_out, own_fc1, own_fc2):
        high = low + shards * target.shape[1]
        own(target, biases[:, low:high])
        low = high
    whole = share[...].reshape(groups * count, share.shape[2])
    left = whole[:, span : span + cols]
    total_mod[...] = dot_tn(left, whole[:, :span])


def call(kernel, shards, inside, outside, outs, outside_outs, scratch, flops):
    vmem = pl.BlockSpec(memory_space=pltpu.VMEM)
    anywhere = pl.BlockSpec(memory_space=pl.ANY)
    moved = sum(value.size * value.dtype.itemsize for value in inside + outside)
    moved += sum(value.size * value.dtype.itemsize for value in outs + outside_outs)
    return pl.pallas_call(
        functools.partial(kernel, shards),
        out_shape=outs + outside_outs,
        in_specs=[vmem] * len(inside) + [anywhere] * len(outside),
        out_specs=[vmem] * len(outs) + [anywhere] * len(outside_outs),
        scratch_shapes=scratch,
        cost_estimate=pl.CostEstimate(flops=flops, bytes_accessed=moved, transcendentals=0),
        compiler_params=pltpu.CompilerParams(vmem_limit_bytes=56 << 20),
    )(*inside, *outside)


def shape(dims, dtype):
    return jax.ShapeDtypeStruct(dims, dtype)


def body(
    shards,
    replicas,
    tokens,
    cond,
    cot,
    w_mod,
    b_mod,
    w_qkv,
    b_qv,
    w_out,
    b_out,
    w_fc1,
    b_fc1,
    w_fc2,
    b_fc2,
):
    place = lax.axis_index("shard")
    core = lax.axis_index("replica") % 2
    rows, width = tokens.shape
    mod_rows = w_mod.shape[0]
    inner = w_fc1.shape[1]

    def half_of(weight):
        half = weight.shape[0] // 2
        return lax.dynamic_slice_in_dim(weight, core * half, half, 0)

    all_qkvo = Gather(jnp.concatenate([half_of(w_qkv), half_of(w_out)], 1), shards, replicas)
    all_fc1 = Gather(half_of(w_fc1), shards, replicas)
    all_fc2 = Gather(half_of(w_fc2), shards, replicas)
    cond_f = cond.astype(F32)
    cond_act = jax.nn.silu(cond_f).astype(BF16)
    biases = [b_qv, b_out, b_fc1, b_fc2]
    note = jnp.concatenate([cond_act[0]] + biases)[None]
    got = all_qkvo.send(1, all_qkvo.operands(1))
    came = [hop(note, "shard", shards, number) for number in range(1, shards)]
    got = gate(got, *came)
    all_qkvo.hold(1, got)
    notes = jnp.concatenate([note] + gate(came, *got), 0)
    group_cols = lax.dynamic_slice_in_dim(notes[:, :width], place * mod_rows, mod_rows, 1)
    partial = dot_nn(group_cols, w_mod)
    own_bias = lax.dynamic_update_slice(
        jnp.zeros((6 * width,), F32), b_mod.astype(F32), (place * b_mod.shape[0],)
    )
    partial = partial + own_bias
    def rest(gather, behind):
        for depth in range(2, gather.depths + 1):
            got = gather.send(depth, behind if depth == 2 else gather.operands(depth))
            if depth < gather.depths:
                gather.hold(depth, got)
        return got

    came = [hop(partial[number : number + 1], "shard", shards, number) for number in range(1, shards)]
    came, got = together(came, rest(all_qkvo, all_qkvo.operands(2)))
    all_qkvo.hold(all_qkvo.depths, got)
    mod = partial[0:1]
    for row in came:
        mod = mod + row
    bias_rows = xor_rows(gate([notes], mod)[0][:, width:].astype(F32), place)
    full_bias = []
    start = 0
    for piece in biases:
        full_bias.append(bias_rows[:, start : start + piece.shape[0]].reshape(1, -1))
        start += piece.shape[0]
    bias_qv, bias_out, bias_fc1, bias_fc2 = full_bias

    pieces_qkvo = all_qkvo.pieces()
    ahead = gate(all_fc1.operands(1), *got)
    got_fc1 = all_fc1.send(1, ahead)
    tokens_in = after(tokens, *ahead)

    pieces = piece_total(shards)
    sems = pltpu.SemaphoreType.DMA
    qkvo_scratch = [pltpu.VMEM((width, 4 * width), BF16)]
    fc1_scratch = [pltpu.VMEM((width, inner), BF16)]
    fc2_scratch = [pltpu.VMEM((inner, width), BF16)]
    half = mod_rows // 2
    half_inner = w_fc2.shape[0] // 2
    chunks = inner // width

    modul_a, qkv, attended, lse, branch_a, middle, modul_b = call(
        attend_kernel,
        shards,
        [tokens_in, mod, bias_qv, bias_out],
        [w_qkv, w_out] + pieces_qkvo,
        [
            shape((rows, width), BF16),
            shape((rows, 3 * width), BF16),
            shape((rows, width), BF16),
            shape((rows, 2 * HEAD), F32),
            shape((rows, width), F32),
            shape((rows, width), F32),
            shape((rows, width), BF16),
        ],
        [],
        qkvo_scratch + [sems((pieces + 2,))],
        10**11,
    )
    got_fc1, [modul_b, middle] = together(got_fc1, [modul_b, middle])
    all_fc1.hold(1, got_fc1)
    got = rest(all_fc1, all_fc1.operands(2))
    ahead = gate(all_fc2.operands(1), *got)
    all_fc1.hold(all_fc1.depths, got)
    pieces_fc1 = all_fc1.pieces()
    got_fc2 = all_fc2.send(1, ahead)
    hidden, slope, *outs = call(
        hidden_kernel,
        shards,
        [after(modul_b, *ahead), cot, mod, bias_fc1],
        [w_fc1] + pieces_fc1,
        [shape((rows, inner), BF16), shape((rows, inner), F32)],
        [shape((shards, half_inner, width), BF16)] * 2,
        fc1_scratch
        + [pltpu.VMEM((shards, 2 * half_inner, width), BF16)]
        + [sems((pieces + 1,)), sems((2 * shards,))],
        10**11,
    )
    got_fc2, [slope, *outs] = together(got_fc2, [slope, *outs])
    all_fc2.hold(1, got_fc2)
    all_fc2.hold(all_fc2.depths, rest(all_fc2, all_fc2.operands(2)))
    pieces_fc2 = all_fc2.pieces()
    red_fc2 = Reduction(outs[0], outs[1], shards, replicas, 1)
    red_fc2.swap()
    low_pre, sum_pre, *outs = call(
        pre_kernel,
        shards,
        [modul_b, cot, mod, slope],
        [w_fc2] + pieces_fc2,
        [shape((rows, inner), BF16), shape((1, inner), F32)],
        [shape((shards, half, inner), BF16)] * 2,
        fc2_scratch
        + fc1_scratch
        + [pltpu.VMEM((width, rows), BF16), sems((pieces + 1,)), sems((2 * shards * chunks,))],
        10**11,
    )
    [red_fc2.came], [low_pre, *outs] = together([red_fc2.came], [low_pre, *outs])
    red_fc1 = Reduction(outs[0], outs[1], shards, replicas, 1)
    red_fc1.swap()
    low_pre = after(low_pre, *red_fc2.ready(0))
    red_fc2.send(0)
    grad_middle, low_branch_a, sum_out, mods_b = call(
        middle_kernel,
        shards,
        [low_pre, cot, mod, middle, branch_a],
        [w_fc1] + pieces_fc1,
        [
            shape((rows, width), F32),
            shape((rows, width), BF16),
            shape((1, width), F32),
            shape((3, width), F32),
        ],
        [],
        fc1_scratch + [sems((pieces + 1,))],
        10**11,
    )
    got, [red_fc1.came], [low_branch_a] = together(
        red_fc2.flying, [red_fc1.came], [low_branch_a]
    )
    red_fc2.land(got)
    stages = len(red_fc2.bits)
    for stage in range(1, stages - 1):
        red_fc2.ready(stage)
        red_fc2.land(red_fc2.send(stage))
    low_branch_a = after(low_branch_a, *red_fc2.ready(stages - 1), *red_fc1.ready(0))
    red_fc2.send(stages - 1)
    red_fc1.send(0)
    low_proj, sum_proj, *outs = call(
        back_kernel,
        shards,
        [low_branch_a, modul_a, qkv, attended, lse],
        [w_qkv, w_out] + pieces_qkvo,
        [shape((rows, 3 * width), BF16), shape((1, 3 * width), F32)],
        [shape((shards, half, 4 * width), BF16)] * 2,
        qkvo_scratch
        + qkvo_scratch
        + [pltpu.VMEM((rows, width), BF16), pltpu.VMEM((width, rows), BF16)]
        + [sems((pieces + 2,)), sems((8 * shards,))],
        10**11,
    )
    got_2, got_1, [low_proj, *outs] = together(
        red_fc2.flying, red_fc1.flying, [low_proj, *outs]
    )
    red_fc2.land(got_2)
    red_fc1.land(got_1)
    red_qkvo = Reduction(outs[0], outs[1], shards, replicas, part_count(shards))
    red_qkvo.swap()
    for stage in range(1, stages - 1):
        red_fc1.ready(stage)
        red_fc1.land(red_fc1.send(stage))
    low_proj = after(low_proj, *red_qkvo.ready(0), *red_fc1.ready(stages - 1), *red_fc2.own())
    red_qkvo.send(0)
    red_fc1.send(stages - 1)
    red_fc2.fold(0)
    grad_tokens, mixed, news = call(
        last_kernel,
        shards,
        [low_proj, tokens, mod, grad_middle, hidden, middle, cot, bias_fc2]
        + [sum_proj, sum_out, sum_pre, mods_b],
        [w_qkv, w_out] + pieces_qkvo + [w_fc2] + pieces_fc2,
        [
            shape((rows, width), F32),
            shape((rows, width), BF16),
            shape((1, 6 * width + 3 * width + inner + width), BF16),
        ],
        [],
        qkvo_scratch + fc2_scratch + [sems((pieces + 2,)), sems((pieces + 1,))],
        10**11,
    )
    got_q, got_1, got_2, [news] = together(
        red_qkvo.flying, red_fc1.flying, red_fc2.flying, [news]
    )
    red_qkvo.land(got_q)
    red_fc1.land(got_1)
    red_fc2.folded(0, got_2)
    for stage in range(1, stages - 1):
        red_qkvo.ready(stage)
        red_qkvo.land(red_qkvo.send(stage))
    steps = red_fc2.rounds()
    count = -(-(shards + 2) // 8) * 8
    mod_span = 6 * width
    share_span = mod_span + 2 * 128 * -(-mod_rows // 256)
    share_steps = replicas.bit_length() - 1

    def mod_chain():
        held = [news]
        flip = 1
        while flip < shards:
            got = yield [(value, "shard", flip) for value in held]
            held += got
            flip *= 2
        *back, share = call(
            share_kernel,
            shards,
            held + [w_mod, group_cols],
            [],
            [shape((1, width), F32)] * shards + [shape((1, count, share_span), BF16)],
            [],
            [pltpu.VMEM((count, share_span), F32)],
            10**8,
        )
        rows = dict(enumerate(back))
        step = 0
        while step < share_steps:
            moving = [(share, "replica", replicas >> (step + 1))]
            half = shards >> (step + 1)
            if half:
                moving += [(rows[half + at], "shard", half) for at in range(half)]
            got = yield moving
            share = jnp.concatenate([share, got[0]], 0)
            for at in range(half):
                rows[at] = rows[at] + got[1 + at]
            step += 1
        while shards >> (step + 1):
            half = shards >> (step + 1)
            got = yield [(rows[half + at], "shard", half) for at in range(half)]
            for at in range(half):
                rows[at] = rows[at] + got[at]
            step += 1
        mod_chain.result = (share, rows[0])

    def send_on(moves):
        return [
            hop(value, axis, shards if axis == "shard" else replicas, flip)
            for value, axis, flip in moves
        ]

    at_1, at_2 = 1, min(2, steps)
    sent_1 = red_fc1.own() + red_fc2.values
    flying_1 = red_fc1.fold(0)
    flying_2 = red_fc2.fold(1) if steps > 1 else []
    red_qkvo.keep = after(red_qkvo.keep, *sent_1)
    sent_q = red_qkvo.ready(stages - 1)
    flying_q = red_qkvo.send(stages - 1)
    [news], flying_1, flying_2, _ = together([news], flying_1, flying_2, sent_q)
    red_fc1.folded(0, flying_1)
    if steps > 1:
        red_fc2.folded(1, flying_2)
    chain = mod_chain()
    moves = next(chain)
    at_q = -1
    while True:
        moves = list(moves)
        values = [value for value, _, _ in moves]
        lanes = [[], []]
        if at_1 < steps:
            lanes[0] = red_fc1.fold(at_1)
        if at_2 < steps:
            lanes[1] = red_fc2.fold(at_2)
        flying_m = send_on(moves)
        sent_b = values + red_fc1.values + red_fc2.values
        if at_q < steps:
            got = gate(flying_q, *sent_b)
            if at_q < 0:
                red_qkvo.land(got)
                red_qkvo.own()
            else:
                red_qkvo.folded(at_q, got)
            at_q += 1
            if at_q < steps:
                flying_q = red_qkvo.fold(at_q)
        lanes[0], lanes[1], flying_m, _ = together(
            lanes[0], lanes[1], flying_m, red_qkvo.values
        )
        if at_1 < steps:
            red_fc1.folded(at_1, lanes[0])
            at_1 += 1
        if at_2 < steps:
            red_fc2.folded(at_2, lanes[1])
            at_2 += 1
        try:
            moves = chain.send(flying_m) if chain else []
        except StopIteration:
            chain = None
            moves = []
        if chain is None and at_1 >= steps and at_2 >= steps and at_q >= steps:
            break
    share, grad_row = mod_chain.result
    _, silu_back = jax.vjp(jax.nn.silu, cond_f)
    grad_cond = silu_back(grad_row)[0]
    total_mod, total_b_mod, *bias_totals = call(
        total_kernel,
        shards,
        [share],
        [],
        [shape((mod_rows, mod_span), F32), shape((1, b_mod.shape[0]), F32)]
        + [shape((1, piece.shape[0]), F32) for piece in biases],
        [],
        [],
        10**8,
    )
    total_b_mod = total_b_mod.reshape(-1)
    bias_totals = [piece.reshape(-1) for piece in bias_totals]

    total_fc2 = red_fc2.finish()
    total_fc1 = red_fc1.finish()
    total_qkvo = red_qkvo.finish()
    return (
        mixed,
        grad_tokens,
        grad_cond,
        total_mod,
        total_b_mod,
        total_qkvo[:, : 3 * width],
        bias_totals[0],
        total_qkvo[:, 3 * width :],
        bias_totals[1],
        total_fc1,
        bias_totals[2],
        total_fc2,
        bias_totals[3],
    )


def solution(mesh):
    shards = mesh.shape["shard"]
    replicas = mesh.shape["replica"]
    both = P(("shard", "replica"), None)
    pairs = (P("shard", None), P("shard")) * 5

    def run(*args):
        return body(shards, replicas, *args)

    return jax.shard_map(
        run,
        mesh=mesh,
        in_specs=(both, both, both) + pairs,
        out_specs=(both, both, both) + pairs,
        check_vma=False,
    )
```

```python
import functools

import jax
import jax.numpy as jnp
from jax import lax
from jax.experimental import pallas as pl
from jax.experimental.pallas import tpu as pltpu
from jax.sharding import PartitionSpec as P

F32 = jnp.float32
BF16 = jnp.bfloat16
HEAD = 64


def dot_nn(left, right):
    return lax.dot_general(left, right, (((1,), (0,)), ((), ())), preferred_element_type=F32)


def dot_tn(left, right):
    return lax.dot_general(left, right, (((0,), (0,)), ((), ())), preferred_element_type=F32)


def dot_nt(left, right):
    return lax.dot_general(left, right, (((1,), (1,)), ((), ())), preferred_element_type=F32)


def layer_norm(values):
    center = values - jnp.mean(values, -1, keepdims=True)
    rstd_val = lax.rsqrt(jnp.mean(center * center, -1, keepdims=True) + 1e-06)
    return (center * rstd_val, rstd_val)


def norm_back(grad_norm, normed, rstd_val):
    return rstd_val * (
        grad_norm
        - jnp.mean(grad_norm, -1, keepdims=True)
        - normed * jnp.mean(grad_norm * normed, -1, keepdims=True)
    )


def hop(value, axis, size, flip):
    return lax.ppermute(value, axis, [(at, at ^ flip) for at in range(size)])


def bits_of(number):
    return [1 << at for at in range(number.bit_length()) if number >> at & 1]


def by_weight(count):
    return sorted(range(1, count), key=lambda number: (bin(number).count("1"), number))


def xor_rows(rows, place):
    count = rows.shape[0]
    flip = 1
    while flip < count:
        swapped = rows.reshape(count // (2 * flip), 2, flip, -1)[:, ::-1].reshape(rows.shape)
        rows = jnp.where((place & flip) != 0, swapped, rows)
        flip *= 2
    return rows


def part_count(shards):
    return max(1, shards.bit_length() - 1)


def piece_layout(shards, width):
    layout = []
    for number in by_weight(shards):
        parts = 1 if len(bits_of(number)) == 1 else part_count(shards)
        span = width // parts
        layout += [(number, at * span, span) for at in range(parts)]
    return layout


def way(number, at):
    ways = bits_of(number)
    return ways[at % len(ways)]


def after(value, *others):
    return lax.optimization_barrier((value,) + others)[0]


def gate(values, *others):
    return list(lax.optimization_barrier(tuple(values) + others)[: len(values)])


class Gather:
    def __init__(self, half, shards, replicas):
        self.shards, self.replicas = shards, replicas
        self.half = half
        self.parts = part_count(shards)
        self.held = {}
        self.depths = shards.bit_length() - 1

    def operands(self, depth):
        span = self.half.shape[1] // self.parts
        if depth == 1:
            return [self.half]
        found = []
        for number in range(1, self.shards):
            if len(bits_of(number)) == depth:
                for at in range(self.parts):
                    source = self.held[number ^ way(number, at)]
                    if isinstance(source, list):
                        found.append(source[at])
                    else:
                        found.append(source[:, at * span : (at + 1) * span])
        return found

    def send(self, depth, operands):
        got = []
        operands = list(operands)
        for number in range(1, self.shards):
            if len(bits_of(number)) == depth:
                if depth == 1:
                    got.append(hop(operands[0], "shard", self.shards, number))
                else:
                    for at in range(self.parts):
                        flip = way(number, at)
                        got.append(hop(operands.pop(0), "shard", self.shards, flip))
        return got

    def hold(self, depth, got):
        got = list(got)
        for number in range(1, self.shards):
            if len(bits_of(number)) == depth:
                if depth == 1:
                    self.held[number] = got.pop(0)
                else:
                    self.held[number] = [got.pop(0) for _ in range(self.parts)]

    def pieces(self):
        flat = []
        for number in by_weight(self.shards):
            piece = self.held[number]
            flat += piece if isinstance(piece, list) else [piece]
        return flat + [hop(piece, "replica", self.replicas, 1) for piece in flat]


class Reduction:
    def __init__(self, keep, send, shards, replicas, chunks):
        self.keep, self.partner = keep, send
        self.shards, self.replicas, self.chunks = shards, replicas, chunks
        self.parts = part_count(shards)
        self.bits = [1 << at for at in range(shards.bit_length() - 1)]
        self.terms = {at: [] for at in range(self.parts)}

    def swap(self):
        self.came = hop(self.partner, "replica", self.replicas, 1)
        return self.came

    def order(self, at):
        return self.bits[at:] + self.bits[:at]

    def total(self, at, stage):
        order = self.order(at)
        span = self.keep.shape[2] // self.parts
        index = [slice(None)] * len(order)
        for bit in order[:stage]:
            index[len(order) - bit.bit_length()] = slice(0, 1)
        if stage < len(order):
            index[len(order) - order[stage].bit_length()] = slice(1, 2)
        index = tuple(index)
        value = None
        for array in (self.keep, self.came):
            cube = array.reshape((2,) * len(order) + array.shape[1:])
            cube = cube[index + (slice(None), slice(at * span, (at + 1) * span))].astype(F32)
            value = cube if value is None else value + cube
        for term in self.terms[at]:
            value = value + term[index].astype(F32)
        return value

    def ready(self, stage):
        self.sent = [self.total(at, stage).astype(BF16) for at in range(self.parts)]
        return self.sent

    def send(self, stage):
        self.flying = []
        for at in range(self.parts):
            piece = self.sent[at]
            got = hop(
                piece.reshape((-1,) + piece.shape[-2:]), "shard", self.shards, self.order(at)[stage]
            )
            self.flying.append(got.reshape(piece.shape))
        return self.flying

    def land(self, got):
        for at in range(self.parts):
            self.terms[at].append(got[at])

    def own(self):
        values = [self.total(at, len(self.bits)) for at in range(self.parts)]
        values = [value.reshape(value.shape[-2:]) for value in values]
        if self.chunks == 1:
            values = [jnp.concatenate(values, 1)]
        self.values = [value.astype(BF16) for value in values]
        return self.values

    def rounds(self):
        return self.replicas // 2 - 1

    def fold(self, at):
        chips = self.replicas // 2
        mid = chips // 2 - 1
        if at < mid:
            links = [(at, at + 1), (chips - 1 - at, chips - 2 - at)]
        elif at == mid:
            links = [(mid, mid + 1), (mid + 1, mid)]
        else:
            out = 2 * mid - at
            links = [(out + 1, out), (chips - 2 - out, chips - 1 - out)]
        pairs = [(2 * low + core, 2 * high + core) for low, high in links for core in range(2)]
        self.flying = [lax.ppermute(value, "replica", pairs) for value in self.values]
        return self.flying

    def folded(self, at, got):
        chips = self.replicas // 2
        mid = chips // 2 - 1
        chip = lax.axis_index("replica") // 2
        if at <= mid:
            self.values = [
                (value.astype(F32) + piece.astype(F32)).astype(BF16)
                for value, piece in zip(self.values, got)
            ]
        else:
            out = 2 * mid - at
            outer = (chip == out) | (chip == chips - 1 - out)
            self.values = [
                jnp.where(outer, piece, value) for value, piece in zip(self.values, got)
            ]
        return self.values

    def finish(self):
        core = lax.axis_index("replica") % 2
        cols = []
        for value in self.values:
            other = hop(value, "replica", self.replicas, 1)
            cols.append(
                jnp.where(
                    core == 1,
                    jnp.concatenate([other, value], 0),
                    jnp.concatenate([value, other], 0),
                )
            )
        whole = cols[0] if len(cols) == 1 else jnp.concatenate(cols, 1)
        return whole.astype(F32)


def together(*groups):
    flat = [value for group in groups for value in group]
    flat = list(lax.optimization_barrier(tuple(flat)))
    found = []
    for group in groups:
        found.append(flat[: len(group)])
        flat = flat[len(group) :]
    return found


def start_fetch(own, pieces, whole, sems, shards):
    place = lax.axis_index("shard")
    core = lax.axis_index("replica") % 2
    total_rows, width = whole.shape
    block = total_rows // shards
    half = block // 2
    copies = []

    def add(source, row, low, cols):
        rows = source.shape[0]
        there = whole.at[pl.ds(pl.multiple_of(row, 16), rows), pl.ds(low, cols)]
        copy = pltpu.make_async_copy(source, there, sems.at[len(copies)])
        copy.start()
        copies.append(copy)

    low = 0
    for part in own:
        cols = part.shape[1]
        add(part, place * block, low, cols)
        low += cols
    layout = piece_layout(shards, width)
    for at, (number, first, cols) in enumerate(layout):
        for side, source in ((core, pieces[at]), (1 - core, pieces[len(layout) + at])):
            add(source, (place ^ number) * block + side * half, first, cols)
    return copies


def start_emit(grad, low, cols, keep, send, sems, shards, copies):
    place = lax.axis_index("shard")
    core = lax.axis_index("replica") % 2
    block = grad.shape[0] // shards
    half = block // 2
    for number in range(shards):
        for side, target in ((core, keep), (1 - core, send)):
            row = pl.multiple_of((place ^ number) * block + side * half, 16)
            copy = pltpu.make_async_copy(
                grad.at[pl.ds(row, half), pl.ds(low, cols)],
                target.at[number, :, pl.ds(low, cols)],
                sems.at[len(copies)],
            )
            copy.start()
            copies.append(copy)


def wait_all(copies):
    for copy in copies:
        copy.wait()


def mod_piece(mod, at, width):
    return mod[:, at * width : (at + 1) * width]


def piece_total(shards):
    return 2 * len(piece_layout(shards, 1 << 20))


def take(refs, count):
    head = refs[:count]
    del refs[:count]
    return head


def gelu_parts(pre):
    scale = 0.7978845608028654
    square = pre * pre
    inner = jnp.tanh(scale * (pre + 0.044715 * (square * pre)))
    value = 0.5 * pre * (1.0 + inner)
    slope = 0.5 * (1.0 + inner) + 0.5 * pre * (1.0 - inner * inner) * (
        scale * (1.0 + 0.134145 * square)
    )
    return value, slope


def attend_kernel(shards, *refs):
    refs = list(refs)
    tokens, mod, bias_qv, bias_out = take(refs, 4)
    own = take(refs, 2)
    pieces = take(refs, piece_total(shards))
    modul_a, qkv, attended, lse, branch_a, middle, modul_b = take(refs, 7)
    weight, sems = refs
    rows, width = tokens.shape
    copies = start_fetch(own, pieces, weight, sems, shards)
    inputs = tokens[...].astype(F32)
    norm_a, _ = layer_norm(inputs)
    mod_val = mod[...]
    modul = (norm_a * (1.0 + mod_piece(mod_val, 1, width)) + mod_piece(mod_val, 0, width)).astype(
        BF16
    )
    modul_a[...] = modul
    wait_all(copies)
    for at in range(3):
        projected = dot_nn(modul, weight[:, at * width : (at + 1) * width])
        if at != 1:
            low = 0 if at == 0 else width
            projected = projected + bias_qv[:, low : low + width]
        qkv[:, at * width : (at + 1) * width] = projected.astype(BF16)
    lane = lax.broadcasted_iota(jnp.int32, (rows, 2 * HEAD), 1)

    def pair(at, lse_all):
        col = pl.multiple_of(at * 2 * HEAD, 2 * HEAD)
        query = qkv[:, pl.ds(col, 2 * HEAD)]
        key = qkv[:, pl.ds(width + col, 2 * HEAD)]
        value = qkv[:, pl.ds(2 * width + col, 2 * HEAD)]
        out = jnp.zeros((rows, 2 * HEAD), F32)
        for side in range(2):
            mask = (lane < HEAD) if side == 0 else (lane >= HEAD)
            scores = dot_nt(jnp.where(mask, query, 0), key) * 0.125
            top = jnp.max(scores, -1, keepdims=True)
            exps = jnp.exp(scores - top)
            total = jnp.sum(exps, -1, keepdims=True)
            probs = (exps / total).astype(BF16)
            out = out + dot_nn(probs, jnp.where(mask, value, 0))
            lse_all = jnp.where(lane == 2 * at + side, top + jnp.log(total), lse_all)
        attended[:, pl.ds(col, 2 * HEAD)] = out.astype(BF16)
        return lse_all

    lse[...] = lax.fori_loop(
        0, width // (2 * HEAD), pair, jnp.zeros((rows, 2 * HEAD), F32)
    )
    branch = dot_nn(attended[...], weight[:, 3 * width :]) + bias_out[...]
    branch_a[...] = branch
    mid = inputs + mod_piece(mod_val, 2, width) * branch
    middle[...] = mid
    norm_b, _ = layer_norm(mid)
    modul_b[...] = (
        norm_b * (1.0 + mod_piece(mod_val, 4, width)) + mod_piece(mod_val, 3, width)
    ).astype(BF16)


def hidden_kernel(shards, *refs):
    refs = list(refs)
    modul_b, cot, mod, bias_fc1 = take(refs, 4)
    own = take(refs, 1)
    pieces = take(refs, piece_total(shards))
    hidden, slope = take(refs, 2)
    keep, send = take(refs, 2)
    weight, grad, sems, out_sems = refs
    rows, width = modul_b.shape
    copies = start_fetch(own, pieces, weight, sems, shards)
    low_branch = (cot[...].astype(F32) * mod_piece(mod[...], 5, width)).astype(BF16)
    modul = modul_b[...]
    wait_all(copies)
    place = lax.axis_index("shard")
    core = lax.axis_index("replica") % 2
    span = weight.shape[1] // shards
    half = span // 2
    outs = []
    for number in range(shards - 1, -1, -1):
        col = pl.multiple_of((place ^ number) * span, 128)
        pre = dot_nn(modul, weight[:, pl.ds(col, span)]) + bias_fc1[:, pl.ds(col, span)]
        value, rate = gelu_parts(pre)
        value = value.astype(BF16)
        hidden[:, pl.ds(col, span)] = value
        slope[:, pl.ds(col, span)] = rate
        grad[number] = dot_tn(value, low_branch).astype(BF16)
        for side, target in ((core, keep), (1 - core, send)):
            row = pl.multiple_of(side * half, 16)
            copy = pltpu.make_async_copy(
                grad.at[number, pl.ds(row, half), :], target.at[number], out_sems.at[len(outs)]
            )
            copy.start()
            outs.append(copy)
    wait_all(outs)


def pre_kernel(shards, *refs):
    refs = list(refs)
    modul_b, cot, mod, slope = take(refs, 4)
    own = take(refs, 1)
    pieces = take(refs, piece_total(shards))
    low_pre, sum_pre = take(refs, 2)
    keep, send = take(refs, 2)
    weight, grad, turned, sems, out_sems = refs
    rows, width = modul_b.shape
    copies = start_fetch(own, pieces, weight, sems, shards)
    low_branch = (cot[...].astype(F32) * mod_piece(mod[...], 5, width)).astype(BF16)
    turned[...] = modul_b[...].T
    wait_all(copies)

    outs = []
    for col in range(0, weight.shape[0], width):
        cols = slice(col, col + width)
        grad_pre = dot_nt(low_branch, weight[cols, :]) * slope[:, cols]
        sum_pre[:, cols] = jnp.sum(grad_pre, 0, keepdims=True)
        low = grad_pre.astype(BF16)
        low_pre[:, cols] = low
        grad[:, cols] = dot_nn(turned[...], low).astype(BF16)
        start_emit(grad, col, width, keep, send, out_sems, shards, outs)
    wait_all(outs)


def middle_kernel(shards, *refs):
    refs = list(refs)
    low_pre, cot, mod, middle, branch_a = take(refs, 5)
    own = take(refs, 1)
    pieces = take(refs, piece_total(shards))
    grad_middle, low_branch_a, sum_out, grad_mods = take(refs, 4)
    weight, sems = refs
    rows, width = middle.shape
    copies = start_fetch(own, pieces, weight, sems, shards)
    mod_val = mod[...]
    norm_b, rstd_b = layer_norm(middle[...])
    wait_all(copies)
    grad_modul = dot_nt(low_pre[...], weight[...])
    grad_mods[0:1, :] = jnp.sum(grad_modul, 0, keepdims=True)
    grad_mods[1:2, :] = jnp.sum(grad_modul * norm_b, 0, keepdims=True)
    grad_mid = cot[...].astype(F32) + norm_back(
        grad_modul * (1.0 + mod_piece(mod_val, 4, width)), norm_b, rstd_b
    )
    grad_middle[...] = grad_mid
    grad_mods[2:3, :] = jnp.sum(grad_mid * branch_a[...], 0, keepdims=True)
    grad_branch = grad_mid * mod_piece(mod_val, 2, width)
    sum_out[...] = jnp.sum(grad_branch, 0, keepdims=True)
    low_branch_a[...] = grad_branch.astype(BF16)


def back_kernel(shards, *refs):
    refs = list(refs)
    low_branch_a, modul_a, qkv, attended, lse = take(refs, 5)
    own = take(refs, 2)
    pieces = take(refs, piece_total(shards))
    low_proj, sum_proj = take(refs, 2)
    keep, send = take(refs, 2)
    weight, grad, grad_att, turned, sems, out_sems = refs
    rows, width = modul_a.shape
    copies = start_fetch(own, pieces, weight, sems, shards)
    low_branch = low_branch_a[...]
    outs = []
    turned[...] = attended[...].T
    grad[:, 3 * width :] = dot_nn(turned[...], low_branch).astype(BF16)
    start_emit(grad, 3 * width, width, keep, send, out_sems, shards, outs)
    turned[...] = modul_a[...].T
    wait_all(copies)
    grad_att[...] = dot_nt(low_branch, weight[:, 3 * width :]).astype(BF16)
    lane = lax.broadcasted_iota(jnp.int32, (rows, 2 * HEAD), 1)
    lse_val = lse[...]

    def pair(at, carry):
        col = pl.multiple_of(at * 2 * HEAD, 2 * HEAD)
        query = qkv[:, pl.ds(col, 2 * HEAD)]
        key = qkv[:, pl.ds(width + col, 2 * HEAD)]
        value = qkv[:, pl.ds(2 * width + col, 2 * HEAD)]
        grad_out = grad_att[:, pl.ds(col, 2 * HEAD)]
        product = grad_out.astype(F32) * attended[:, pl.ds(col, 2 * HEAD)].astype(F32)
        grad_q = jnp.zeros((rows, 2 * HEAD), F32)
        grad_k = jnp.zeros((rows, 2 * HEAD), F32)
        grad_v = jnp.zeros((rows, 2 * HEAD), F32)
        for side in range(2):
            mask = (lane < HEAD) if side == 0 else (lane >= HEAD)
            query_m = jnp.where(mask, query, 0)
            grad_m = jnp.where(mask, grad_out, 0)
            scores = dot_nt(query_m, key) * 0.125
            log_total = jnp.sum(
                jnp.where(lane == 2 * at + side, lse_val, 0.0), -1, keepdims=True
            )
            probs = jnp.exp(scores - log_total)
            delta = jnp.sum(jnp.where(mask, product, 0.0), -1, keepdims=True)
            grad_scores = (probs * (dot_nt(grad_m, value) - delta) * 0.125).astype(BF16)
            grad_v = grad_v + dot_tn(probs.astype(BF16), grad_m)
            grad_q = grad_q + dot_nn(grad_scores, jnp.where(mask, key, 0))
            grad_k = grad_k + dot_tn(grad_scores, query_m)
        for part, piece in enumerate((grad_q, grad_k, grad_v)):
            there = pl.multiple_of(part * width + col, 2 * HEAD)
            sum_proj[:, pl.ds(there, 2 * HEAD)] = jnp.sum(piece, 0, keepdims=True)
            low_proj[:, pl.ds(there, 2 * HEAD)] = piece.astype(BF16)
        return carry

    lax.fori_loop(0, width // (2 * HEAD), pair, 0, unroll=2)
    for at in range(3):
        cols = slice(at * width, (at + 1) * width)
        grad[:, cols] = dot_nn(turned[...], low_proj[:, cols]).astype(BF16)
        start_emit(grad, at * width, width, keep, send, out_sems, shards, outs)
    wait_all(outs)


def tokens_kernel(shards, *refs):
    refs = list(refs)
    low_proj, tokens, mod, grad_middle = take(refs, 4)
    own = take(refs, 2)
    pieces = take(refs, piece_total(shards))
    grad_tokens, grad_mods = take(refs, 2)
    weight, sems = refs
    rows, width = tokens.shape
    copies = start_fetch(own, pieces, weight, sems, shards)
    norm_a, rstd_a = layer_norm(tokens[...].astype(F32))
    wait_all(copies)
    grad_modul = dot_nt(low_proj[...], weight[:, : 3 * width])
    grad_mods[0:1, :] = jnp.sum(grad_modul, 0, keepdims=True)
    grad_mods[1:2, :] = jnp.sum(grad_modul * norm_a, 0, keepdims=True)
    grad_tokens[...] = grad_middle[...] + norm_back(
        grad_modul * (1.0 + mod_piece(mod[...], 1, width)), norm_a, rstd_a
    )


def mixed_kernel(shards, *refs):
    refs = list(refs)
    hidden, mod, middle, cot, bias_fc2 = take(refs, 5)
    mods_a, mods_b, sum_proj, sum_out, sum_pre = take(refs, 5)
    own = take(refs, 1)
    pieces = take(refs, piece_total(shards))
    mixed, news = take(refs, 2)
    weight, sems = refs
    rows, width = middle.shape
    copies = start_fetch(own, pieces, weight, sems, shards)
    gate_b = mod_piece(mod[...], 5, width)
    grad_out = cot[...].astype(F32)
    wait_all(copies)
    branch_b = dot_nn(hidden[...], weight[...]) + bias_fc2[...]
    mixed[...] = (middle[...] + gate_b * branch_b).astype(BF16)
    sums = [mods_a[0:1, :], mods_a[1:2, :], mods_b[2:3, :], mods_b[0:1, :], mods_b[1:2, :]]
    sums.append(jnp.sum(grad_out * branch_b, 0, keepdims=True))
    sums += [sum_proj[:, :width], sum_proj[:, 2 * width :], sum_out[...], sum_pre[...]]
    sums.append(jnp.sum(grad_out * gate_b, 0, keepdims=True))
    low = 0
    for piece in sums:
        news[:, low : low + piece.shape[1]] = piece.astype(BF16)
        low += piece.shape[1]


def share_kernel(shards, *refs):
    refs = list(refs)
    news = take(refs, shards)
    w_mod, group_cols = take(refs, 2)
    back = take(refs, shards)
    share, rows_ref = refs
    span = w_mod.shape[1]
    cols = w_mod.shape[0]
    rows_ref[...] = jnp.zeros_like(rows_ref)
    biases = jnp.zeros((1, news[0].shape[1] - span), F32)
    for at in range(shards):
        rows_ref[at : at + 1, :span] = news[at][:, :span].astype(F32)
        biases = biases + news[at][:, span:].astype(F32)
    low = rows_ref[:, :span].astype(BF16)
    rows_back = dot_nt(low, w_mod[...])
    for at in range(shards):
        for owner in range(shards):
            back[at][:, owner * cols : (owner + 1) * cols] = jnp.where(
                lax.axis_index("shard") == owner, rows_back[at : at + 1, :], 0.0
            )
    rows_ref[:shards, span : span + cols] = group_cols[...].astype(F32)
    part = biases.shape[1] // 2
    for at in range(2):
        rows_ref[shards + at : shards + at + 1, :part] = biases[:, at * part : (at + 1) * part]
    share[0] = rows_ref[...].astype(BF16)


def total_kernel(shards, *refs):
    share, total_mod, own_mod, own_qv, own_out, own_fc1, own_fc2 = refs
    cols, span = total_mod.shape
    groups, count, _ = share.shape
    row = lax.broadcasted_iota(jnp.int32, (count, 1), 0)
    total = jnp.zeros((count, share.shape[2]), F32)
    for at in range(groups):
        total = total + share[at].astype(F32)
    place = lax.axis_index("shard")

    def own(target, values):
        size = target.shape[0]
        found = jnp.zeros((1, size), F32)
        for at in range(shards):
            found = jnp.where(place == at, values[:, at * size : (at + 1) * size], found)
        target[...] = found[0]

    own(own_mod, jnp.sum(jnp.where(row < shards, total[:, :span], 0.0), 0, keepdims=True))
    part = shards * (own_qv.shape[0] + own_out.shape[0] + own_fc1.shape[0] + own_fc2.shape[0]) // 2
    biases = jnp.concatenate(
        [total[shards : shards + 1, :part], total[shards + 1 : shards + 2, :part]], 1
    )
    low = 0
    for target in (own_qv, own_out, own_fc1, own_fc2):
        high = low + shards * target.shape[0]
        own(target, biases[:, low:high])
        low = high
    whole = share[...].reshape(groups * count, share.shape[2])
    left = whole[:, span : span + cols]
    total_mod[...] = dot_tn(left, whole[:, :span])


def call(kernel, shards, inside, outside, outs, outside_outs, scratch, flops):
    vmem = pl.BlockSpec(memory_space=pltpu.VMEM)
    anywhere = pl.BlockSpec(memory_space=pl.ANY)
    moved = sum(value.size * value.dtype.itemsize for value in inside + outside)
    moved += sum(value.size * value.dtype.itemsize for value in outs + outside_outs)
    return pl.pallas_call(
        functools.partial(kernel, shards),
        out_shape=outs + outside_outs,
        in_specs=[vmem] * len(inside) + [anywhere] * len(outside),
        out_specs=[vmem] * len(outs) + [anywhere] * len(outside_outs),
        scratch_shapes=scratch,
        cost_estimate=pl.CostEstimate(flops=flops, bytes_accessed=moved, transcendentals=0),
        compiler_params=pltpu.CompilerParams(vmem_limit_bytes=56 << 20),
    )(*inside, *outside)


def shape(dims, dtype):
    return jax.ShapeDtypeStruct(dims, dtype)


def body(
    shards,
    replicas,
    tokens,
    cond,
    cot,
    w_mod,
    b_mod,
    w_qkv,
    b_qv,
    w_out,
    b_out,
    w_fc1,
    b_fc1,
    w_fc2,
    b_fc2,
):
    place = lax.axis_index("shard")
    core = lax.axis_index("replica") % 2
    rows, width = tokens.shape
    mod_rows = w_mod.shape[0]
    inner = w_fc1.shape[1]

    def half_of(weight):
        half = weight.shape[0] // 2
        return lax.dynamic_slice_in_dim(weight, core * half, half, 0)

    all_qkvo = Gather(jnp.concatenate([half_of(w_qkv), half_of(w_out)], 1), shards, replicas)
    all_fc1 = Gather(half_of(w_fc1), shards, replicas)
    all_fc2 = Gather(half_of(w_fc2), shards, replicas)
    cond_f = cond.astype(F32)
    cond_act = jax.nn.silu(cond_f).astype(BF16)
    biases = [b_qv, b_out, b_fc1, b_fc2]
    note = jnp.concatenate([cond_act[0]] + biases)[None]
    got = all_qkvo.send(1, all_qkvo.operands(1))
    came = [hop(note, "shard", shards, number) for number in range(1, shards)]
    got = gate(got, *came)
    all_qkvo.hold(1, got)
    notes = jnp.concatenate([note] + gate(came, *got), 0)
    group_cols = lax.dynamic_slice_in_dim(notes[:, :width], place * mod_rows, mod_rows, 1)
    partial = dot_nn(group_cols, w_mod)
    own_bias = lax.dynamic_update_slice(
        jnp.zeros((6 * width,), F32), b_mod.astype(F32), (place * b_mod.shape[0],)
    )
    partial = partial + own_bias
    def rest(gather, behind):
        for depth in range(2, gather.depths + 1):
            got = gather.send(depth, behind if depth == 2 else gather.operands(depth))
            if depth < gather.depths:
                gather.hold(depth, got)
        return got

    came = [hop(partial[number : number + 1], "shard", shards, number) for number in range(1, shards)]
    got = rest(all_qkvo, all_qkvo.operands(2))
    all_qkvo.hold(all_qkvo.depths, got)
    mod = partial[0:1]
    for row in came:
        mod = mod + row
    bias_rows = xor_rows(gate([notes], partial)[0][:, width:].astype(F32), place)
    full_bias = []
    start = 0
    for piece in biases:
        full_bias.append(bias_rows[:, start : start + piece.shape[0]].reshape(1, -1))
        start += piece.shape[0]
    bias_qv, bias_out, bias_fc1, bias_fc2 = full_bias

    pieces_qkvo = all_qkvo.pieces()
    ahead = gate(all_fc1.operands(1), *got)
    got_fc1 = all_fc1.send(1, ahead)
    tokens_in = after(tokens, *ahead)

    pieces = piece_total(shards)
    sems = pltpu.SemaphoreType.DMA
    qkvo_scratch = [pltpu.VMEM((width, 4 * width), BF16)]
    fc1_scratch = [pltpu.VMEM((width, inner), BF16)]
    fc2_scratch = [pltpu.VMEM((inner, width), BF16)]
    half = mod_rows // 2
    half_inner = w_fc2.shape[0] // 2
    chunks = inner // width

    modul_a, qkv, attended, lse, branch_a, middle, modul_b = call(
        attend_kernel,
        shards,
        [tokens_in, mod, bias_qv, bias_out],
        [w_qkv, w_out] + pieces_qkvo,
        [
            shape((rows, width), BF16),
            shape((rows, 3 * width), BF16),
            shape((rows, width), BF16),
            shape((rows, 2 * HEAD), F32),
            shape((rows, width), F32),
            shape((rows, width), F32),
            shape((rows, width), BF16),
        ],
        [],
        qkvo_scratch + [sems((pieces + 2,))],
        10**11,
    )
    got_fc1, [modul_b, middle] = together(got_fc1, [modul_b, middle])
    all_fc1.hold(1, got_fc1)
    got = rest(all_fc1, all_fc1.operands(2))
    ahead = gate(all_fc2.operands(1), *got)
    all_fc1.hold(all_fc1.depths, got)
    pieces_fc1 = all_fc1.pieces()
    got_fc2 = all_fc2.send(1, ahead)
    hidden, slope, *outs = call(
        hidden_kernel,
        shards,
        [after(modul_b, *ahead), cot, mod, bias_fc1],
        [w_fc1] + pieces_fc1,
        [shape((rows, inner), BF16), shape((rows, inner), F32)],
        [shape((shards, half_inner, width), BF16)] * 2,
        fc1_scratch
        + [pltpu.VMEM((shards, 2 * half_inner, width), BF16)]
        + [sems((pieces + 1,)), sems((2 * shards,))],
        10**11,
    )
    got_fc2, [slope, *outs] = together(got_fc2, [slope, *outs])
    all_fc2.hold(1, got_fc2)
    all_fc2.hold(all_fc2.depths, rest(all_fc2, all_fc2.operands(2)))
    pieces_fc2 = all_fc2.pieces()
    red_fc2 = Reduction(outs[0], outs[1], shards, replicas, 1)
    red_fc2.swap()
    stages = len(red_fc2.bits)
    steps = red_fc2.rounds()
    slope = after(slope, *red_fc2.ready(0))
    red_fc2.send(0)
    low_pre, sum_pre, *outs = call(
        pre_kernel,
        shards,
        [modul_b, cot, mod, slope],
        [w_fc2] + pieces_fc2,
        [shape((rows, inner), BF16), shape((1, inner), F32)],
        [shape((shards, half, inner), BF16)] * 2,
        fc2_scratch
        + fc1_scratch
        + [pltpu.VMEM((width, rows), BF16), sems((pieces + 1,)), sems((2 * shards * chunks,))],
        10**11,
    )
    got, [low_pre, *outs] = together(red_fc2.flying, [low_pre, *outs])
    red_fc2.land(got)
    red_fc1 = Reduction(outs[0], outs[1], shards, replicas, 1)
    red_fc1.swap()
    for stage in range(1, stages - 1):
        red_fc2.ready(stage)
        red_fc2.land(red_fc2.send(stage))
    low_pre = after(low_pre, *red_fc2.ready(stages - 1))
    red_fc2.send(stages - 1)
    grad_middle, low_branch_a, sum_out, mods_b = call(
        middle_kernel,
        shards,
        [low_pre, cot, mod, middle, branch_a],
        [w_fc1] + pieces_fc1,
        [
            shape((rows, width), F32),
            shape((rows, width), BF16),
            shape((1, width), F32),
            shape((3, width), F32),
        ],
        [],
        fc1_scratch + [sems((pieces + 1,))],
        10**11,
    )
    got, [red_fc1.came], [low_branch_a] = together(
        red_fc2.flying, [red_fc1.came], [low_branch_a]
    )
    red_fc2.land(got)
    low_branch_a = after(low_branch_a, *red_fc1.ready(0), *red_fc2.own())
    red_fc1.send(0)
    red_fc2.fold(0)
    low_proj, sum_proj, *outs = call(
        back_kernel,
        shards,
        [low_branch_a, modul_a, qkv, attended, lse],
        [w_qkv, w_out] + pieces_qkvo,
        [shape((rows, 3 * width), BF16), shape((1, 3 * width), F32)],
        [shape((shards, half, 4 * width), BF16)] * 2,
        qkvo_scratch
        + qkvo_scratch
        + [pltpu.VMEM((rows, width), BF16), pltpu.VMEM((width, rows), BF16)]
        + [sems((pieces + 2,)), sems((8 * shards,))],
        10**11,
    )
    got_2, got_1, [low_proj, *outs] = together(
        red_fc2.flying, red_fc1.flying, [low_proj, *outs]
    )
    red_fc2.folded(0, got_2)
    red_fc1.land(got_1)
    red_qkvo = Reduction(outs[0], outs[1], shards, replicas, part_count(shards))
    red_qkvo.swap()
    for stage in range(1, stages - 1):
        red_fc1.ready(stage)
        red_fc1.land(red_fc1.send(stage))
    low_proj = after(low_proj, *red_qkvo.ready(0), *red_fc1.ready(stages - 1), *red_fc2.values)
    red_qkvo.send(0)
    red_fc1.send(stages - 1)
    flying_2 = red_fc2.fold(1) if steps > 1 else []
    grad_tokens, mods_a = call(
        tokens_kernel,
        shards,
        [low_proj, tokens, mod, grad_middle],
        [w_qkv, w_out] + pieces_qkvo,
        [shape((rows, width), F32), shape((2, width), F32)],
        [],
        qkvo_scratch + [sems((pieces + 2,))],
        10**11,
    )
    got_q, got_1, got_2, [mods_a] = together(
        red_qkvo.flying, red_fc1.flying, flying_2, [mods_a]
    )
    red_qkvo.land(got_q)
    red_fc1.land(got_1)
    if steps > 1:
        red_fc2.folded(1, got_2)
    for stage in range(1, stages - 1):
        red_qkvo.ready(stage)
        red_qkvo.land(red_qkvo.send(stage))
    sent_q = red_qkvo.ready(stages - 1)
    red_qkvo.send(stages - 1)
    red_fc1.own()
    red_fc1.fold(0)
    flying_2 = red_fc2.fold(2) if steps > 2 else []
    mods_a = after(mods_a, *sent_q, *red_fc1.values, *red_fc2.values)
    mixed, news = call(
        mixed_kernel,
        shards,
        [hidden, mod, middle, cot, bias_fc2, mods_a, mods_b, sum_proj, sum_out, sum_pre],
        [w_fc2] + pieces_fc2,
        [
            shape((rows, width), BF16),
            shape((1, 6 * width + 3 * width + inner + width), BF16),
        ],
        [],
        fc2_scratch + [sems((pieces + 1,))],
        10**11,
    )
    got_q, got_1, got_2, [news] = together(
        red_qkvo.flying, red_fc1.flying, flying_2, [news]
    )
    red_qkvo.land(got_q)
    red_fc1.folded(0, got_1)
    if steps > 2:
        red_fc2.folded(2, got_2)

    red_qkvo.own()

    count = -(-(shards + 2) // 8) * 8
    mod_span = 6 * width
    share_span = mod_span + 2 * 128 * -(-mod_rows // 256)
    share_steps = replicas.bit_length() - 1

    def mod_chain():
        got = yield [(news, "shard", number) for number in range(1, shards)]
        held = [news] + got
        *back, share = call(
            share_kernel,
            shards,
            held + [w_mod, group_cols],
            [],
            [shape((1, width), F32)] * shards + [shape((1, count, share_span), BF16)],
            [],
            [pltpu.VMEM((count, share_span), F32)],
            10**11,
        )
        share, *back = yield [(value, None, 0) for value in [share, *back]]
        rows = dict(enumerate(back))
        step = 0
        while step < share_steps:
            moving = [(share, "replica", replicas >> (step + 1))]
            half = shards >> (step + 1)
            if half:
                moving += [(rows[half + at], "shard", half) for at in range(half)]
            got = yield moving
            share = jnp.concatenate([share, got[0]], 0)
            for at in range(half):
                rows[at] = rows[at] + got[1 + at]
            step += 1
        while shards >> (step + 1):
            half = shards >> (step + 1)
            got = yield [(rows[half + at], "shard", half) for at in range(half)]
            for at in range(half):
                rows[at] = rows[at] + got[at]
            step += 1
        mod_chain.result = (share, rows[0])

    def send_on(moves):
        return [
            hop(value, axis, shards if axis == "shard" else replicas, flip) if axis else value
            for value, axis, flip in moves
        ]

    chain = mod_chain()
    moves = list(next(chain))
    lanes = {red_qkvo: 0, red_fc1: 1, red_fc2: min(3, steps)}
    while chain or min(lanes.values()) < steps:
        moving = [lane for lane in lanes if lanes[lane] < steps]
        groups = [lane.fold(lanes[lane]) for lane in moving]
        groups = together(*groups, send_on(moves))
        for lane, got in zip(moving, groups):
            lane.folded(lanes[lane], got)
            lanes[lane] += 1
        moves = []
        if chain:
            try:
                moves = list(chain.send(groups[-1]))
            except StopIteration:
                chain = None
    share, grad_row = mod_chain.result
    _, silu_back = jax.vjp(jax.nn.silu, cond_f)
    grad_cond = silu_back(grad_row)[0]
    total_mod, total_b_mod, *bias_totals = call(
        total_kernel,
        shards,
        [share],
        [],
        [shape((mod_rows, mod_span), F32), shape(b_mod.shape, F32)]
        + [shape(piece.shape, F32) for piece in biases],
        [],
        [],
        10**8,
    )

    total_fc2 = red_fc2.finish()
    total_fc1 = red_fc1.finish()
    total_qkvo = red_qkvo.finish()
    return (
        mixed,
        grad_tokens,
        grad_cond,
        total_mod,
        total_b_mod,
        total_qkvo[:, : 3 * width],
        bias_totals[0],
        total_qkvo[:, 3 * width :],
        bias_totals[1],
        total_fc1,
        bias_totals[2],
        total_fc2,
        bias_totals[3],
    )


def solution(mesh):
    shards = mesh.shape["shard"]
    replicas = mesh.shape["replica"]
    both = P(("shard", "replica"), None)
    pairs = (P("shard", None), P("shard")) * 5

    def run(*args):
        return body(shards, replicas, *args)

    return jax.shard_map(
        run,
        mesh=mesh,
        in_specs=(both, both, both) + pairs,
        out_specs=(both, both, both) + pairs,
        check_vma=False,
    )
```

```python
import functools

import jax
import jax.numpy as jnp
from jax import lax
from jax.experimental import pallas as pl
from jax.experimental.pallas import tpu as pltpu
from jax.sharding import PartitionSpec as P

F32 = jnp.float32
BF16 = jnp.bfloat16
HEAD = 64


def dot_nn(left, right):
    return lax.dot_general(left, right, (((1,), (0,)), ((), ())), preferred_element_type=F32)


def dot_tn(left, right):
    return lax.dot_general(left, right, (((0,), (0,)), ((), ())), preferred_element_type=F32)


def dot_nt(left, right):
    return lax.dot_general(left, right, (((1,), (1,)), ((), ())), preferred_element_type=F32)


def layer_norm(values):
    center = values - jnp.mean(values, -1, keepdims=True)
    rstd_val = lax.rsqrt(jnp.mean(center * center, -1, keepdims=True) + 1e-06)
    return (center * rstd_val, rstd_val)


def norm_back(grad_norm, normed, rstd_val):
    return rstd_val * (
        grad_norm
        - jnp.mean(grad_norm, -1, keepdims=True)
        - normed * jnp.mean(grad_norm * normed, -1, keepdims=True)
    )


def hop(value, axis, size, flip):
    return lax.ppermute(value, axis, [(at, at ^ flip) for at in range(size)])


def bits_of(number):
    return [1 << at for at in range(number.bit_length()) if number >> at & 1]


def by_weight(count):
    return sorted(range(1, count), key=lambda number: (bin(number).count("1"), number))


def xor_rows(rows, place):
    count = rows.shape[0]
    flip = 1
    while flip < count:
        swapped = rows.reshape(count // (2 * flip), 2, flip, -1)[:, ::-1].reshape(rows.shape)
        rows = jnp.where((place & flip) != 0, swapped, rows)
        flip *= 2
    return rows


def part_count(shards):
    return max(1, shards.bit_length() - 1)


def piece_layout(shards, width):
    layout = []
    for number in by_weight(shards):
        parts = 1 if len(bits_of(number)) == 1 else part_count(shards)
        span = width // parts
        layout += [(number, at * span, span) for at in range(parts)]
    return layout


def way(number, at):
    ways = bits_of(number)
    return ways[at % len(ways)]


def after(value, *others):
    return lax.optimization_barrier((value,) + others)[0]


def gate(values, *others):
    return list(lax.optimization_barrier(tuple(values) + others)[: len(values)])


class Gather:
    def __init__(self, half, shards, replicas):
        self.shards, self.replicas = shards, replicas
        self.half = half
        self.parts = part_count(shards)
        self.held = {}
        self.depths = shards.bit_length() - 1

    def operands(self, depth):
        span = self.half.shape[1] // self.parts
        if depth == 1:
            return [self.half]
        found = []
        for number in range(1, self.shards):
            if len(bits_of(number)) == depth:
                for at in range(self.parts):
                    source = self.held[number ^ way(number, at)]
                    if isinstance(source, list):
                        found.append(source[at])
                    else:
                        found.append(source[:, at * span : (at + 1) * span])
        return found

    def send(self, depth, operands):
        got = []
        operands = list(operands)
        for number in range(1, self.shards):
            if len(bits_of(number)) == depth:
                if depth == 1:
                    got.append(hop(operands[0], "shard", self.shards, number))
                else:
                    for at in range(self.parts):
                        flip = way(number, at)
                        got.append(hop(operands.pop(0), "shard", self.shards, flip))
        return got

    def hold(self, depth, got):
        got = list(got)
        for number in range(1, self.shards):
            if len(bits_of(number)) == depth:
                if depth == 1:
                    self.held[number] = got.pop(0)
                else:
                    self.held[number] = [got.pop(0) for _ in range(self.parts)]

    def pieces(self):
        flat = []
        for number in by_weight(self.shards):
            piece = self.held[number]
            flat += piece if isinstance(piece, list) else [piece]
        return flat + [hop(piece, "replica", self.replicas, 1) for piece in flat]


class Reduction:
    def __init__(self, keep, send, shards, replicas, chunks):
        self.keep, self.partner = keep, send
        self.shards, self.replicas, self.chunks = shards, replicas, chunks
        self.parts = part_count(shards)
        self.bits = [1 << at for at in range(shards.bit_length() - 1)]
        self.terms = {at: [] for at in range(self.parts)}

    def swap(self):
        self.came = hop(self.partner, "replica", self.replicas, 1)
        return self.came

    def order(self, at):
        return self.bits[at:] + self.bits[:at]

    def total(self, at, stage):
        order = self.order(at)
        span = self.keep.shape[2] // self.parts
        index = [slice(None)] * len(order)
        for bit in order[:stage]:
            index[len(order) - bit.bit_length()] = slice(0, 1)
        if stage < len(order):
            index[len(order) - order[stage].bit_length()] = slice(1, 2)
        index = tuple(index)
        value = None
        for array in (self.keep, self.came):
            cube = array.reshape((2,) * len(order) + array.shape[1:])
            cube = cube[index + (slice(None), slice(at * span, (at + 1) * span))].astype(F32)
            value = cube if value is None else value + cube
        for term in self.terms[at]:
            value = value + term[index].astype(F32)
        return value

    def ready(self, stage):
        self.sent = [self.total(at, stage).astype(BF16) for at in range(self.parts)]
        return self.sent

    def send(self, stage):
        self.flying = []
        for at in range(self.parts):
            piece = self.sent[at]
            got = hop(
                piece.reshape((-1,) + piece.shape[-2:]), "shard", self.shards, self.order(at)[stage]
            )
            self.flying.append(got.reshape(piece.shape))
        return self.flying

    def land(self, got):
        for at in range(self.parts):
            self.terms[at].append(got[at])

    def own(self):
        values = [self.total(at, len(self.bits)) for at in range(self.parts)]
        values = [value.reshape(value.shape[-2:]) for value in values]
        if self.chunks == 1:
            values = [jnp.concatenate(values, 1)]
        self.values = [value.astype(BF16) for value in values]
        return self.values

    def rounds(self):
        return self.replicas // 2 - 1

    def fold(self, at):
        chips = self.replicas // 2
        mid = chips // 2 - 1
        if at < mid:
            links = [(at, at + 1), (chips - 1 - at, chips - 2 - at)]
        elif at == mid:
            links = [(mid, mid + 1), (mid + 1, mid)]
        else:
            out = 2 * mid - at
            links = [(out + 1, out), (chips - 2 - out, chips - 1 - out)]
        pairs = [(2 * low + core, 2 * high + core) for low, high in links for core in range(2)]
        self.flying = [lax.ppermute(value, "replica", pairs) for value in self.values]
        return self.flying

    def folded(self, at, got):
        chips = self.replicas // 2
        mid = chips // 2 - 1
        chip = lax.axis_index("replica") // 2
        if at <= mid:
            self.values = [
                (value.astype(F32) + piece.astype(F32)).astype(BF16)
                for value, piece in zip(self.values, got)
            ]
        else:
            out = 2 * mid - at
            outer = (chip == out) | (chip == chips - 1 - out)
            self.values = [
                jnp.where(outer, piece, value) for value, piece in zip(self.values, got)
            ]
        return self.values

    def finish(self):
        core = lax.axis_index("replica") % 2
        cols = []
        for value in self.values:
            other = hop(value, "replica", self.replicas, 1)
            cols.append(
                jnp.where(
                    core == 1,
                    jnp.concatenate([other, value], 0),
                    jnp.concatenate([value, other], 0),
                )
            )
        whole = cols[0] if len(cols) == 1 else jnp.concatenate(cols, 1)
        return whole.astype(F32)


def together(*groups):
    flat = [value for group in groups for value in group]
    flat = list(lax.optimization_barrier(tuple(flat)))
    found = []
    for group in groups:
        found.append(flat[: len(group)])
        flat = flat[len(group) :]
    return found


def start_fetch(own, pieces, whole, sems, shards):
    place = lax.axis_index("shard")
    core = lax.axis_index("replica") % 2
    total_rows, width = whole.shape
    block = total_rows // shards
    half = block // 2
    copies = []

    def add(source, row, low, cols):
        rows = source.shape[0]
        there = whole.at[pl.ds(pl.multiple_of(row, 16), rows), pl.ds(low, cols)]
        copy = pltpu.make_async_copy(source, there, sems.at[len(copies)])
        copy.start()
        copies.append(copy)

    low = 0
    for part in own:
        cols = part.shape[1]
        add(part, place * block, low, cols)
        low += cols
    layout = piece_layout(shards, width)
    for at, (number, first, cols) in enumerate(layout):
        for side, source in ((core, pieces[at]), (1 - core, pieces[len(layout) + at])):
            add(source, (place ^ number) * block + side * half, first, cols)
    return copies


def start_emit(grad, low, cols, keep, send, sems, shards, copies):
    place = lax.axis_index("shard")
    core = lax.axis_index("replica") % 2
    block = grad.shape[0] // shards
    half = block // 2
    for number in range(shards):
        for side, target in ((core, keep), (1 - core, send)):
            row = pl.multiple_of((place ^ number) * block + side * half, 16)
            copy = pltpu.make_async_copy(
                grad.at[pl.ds(row, half), pl.ds(low, cols)],
                target.at[number, :, pl.ds(low, cols)],
                sems.at[len(copies)],
            )
            copy.start()
            copies.append(copy)


def wait_all(copies):
    for copy in copies:
        copy.wait()


def mod_piece(mod, at, width):
    return mod[:, at * width : (at + 1) * width]


def piece_total(shards):
    return 2 * len(piece_layout(shards, 1 << 20))


def take(refs, count):
    head = refs[:count]
    del refs[:count]
    return head


def gelu_parts(pre):
    scale = 0.7978845608028654
    square = pre * pre
    inner = jnp.tanh(scale * (pre + 0.044715 * (square * pre)))
    value = 0.5 * pre * (1.0 + inner)
    slope = 0.5 * (1.0 + inner) + 0.5 * pre * (1.0 - inner * inner) * (
        scale * (1.0 + 0.134145 * square)
    )
    return value, slope


def attend_kernel(shards, *refs):
    refs = list(refs)
    tokens, mod, bias_qv, bias_out = take(refs, 4)
    own = take(refs, 2)
    pieces = take(refs, piece_total(shards))
    modul_a, qkv, attended, lse, branch_a, middle, modul_b = take(refs, 7)
    weight, sems = refs
    rows, width = tokens.shape
    copies = start_fetch(own, pieces, weight, sems, shards)
    inputs = tokens[...].astype(F32)
    norm_a, _ = layer_norm(inputs)
    mod_val = mod[...]
    modul = (norm_a * (1.0 + mod_piece(mod_val, 1, width)) + mod_piece(mod_val, 0, width)).astype(
        BF16
    )
    modul_a[...] = modul
    wait_all(copies)
    for at in range(3):
        projected = dot_nn(modul, weight[:, at * width : (at + 1) * width])
        if at != 1:
            low = 0 if at == 0 else width
            projected = projected + bias_qv[:, low : low + width]
        qkv[:, at * width : (at + 1) * width] = projected.astype(BF16)
    lane = lax.broadcasted_iota(jnp.int32, (rows, 2 * HEAD), 1)

    def pair(at, lse_all):
        col = pl.multiple_of(at * 2 * HEAD, 2 * HEAD)
        query = qkv[:, pl.ds(col, 2 * HEAD)]
        key = qkv[:, pl.ds(width + col, 2 * HEAD)]
        value = qkv[:, pl.ds(2 * width + col, 2 * HEAD)]
        out = jnp.zeros((rows, 2 * HEAD), F32)
        for side in range(2):
            mask = (lane < HEAD) if side == 0 else (lane >= HEAD)
            scores = dot_nt(jnp.where(mask, query, 0), key) * 0.125
            top = jnp.max(scores, -1, keepdims=True)
            exps = jnp.exp(scores - top)
            total = jnp.sum(exps, -1, keepdims=True)
            probs = (exps / total).astype(BF16)
            out = out + dot_nn(probs, jnp.where(mask, value, 0))
            lse_all = jnp.where(lane == 2 * at + side, top + jnp.log(total), lse_all)
        attended[:, pl.ds(col, 2 * HEAD)] = out.astype(BF16)
        return lse_all

    lse[...] = lax.fori_loop(
        0, width // (2 * HEAD), pair, jnp.zeros((rows, 2 * HEAD), F32)
    )
    branch = dot_nn(attended[...], weight[:, 3 * width :]) + bias_out[...]
    branch_a[...] = branch
    mid = inputs + mod_piece(mod_val, 2, width) * branch
    middle[...] = mid
    norm_b, _ = layer_norm(mid)
    modul_b[...] = (
        norm_b * (1.0 + mod_piece(mod_val, 4, width)) + mod_piece(mod_val, 3, width)
    ).astype(BF16)


def hidden_kernel(shards, *refs):
    refs = list(refs)
    modul_b, cot, mod, bias_fc1 = take(refs, 4)
    own = take(refs, 1)
    pieces = take(refs, piece_total(shards))
    hidden, slope = take(refs, 2)
    keep, send = take(refs, 2)
    weight, grad, sems, out_sems = refs
    rows, width = modul_b.shape
    copies = start_fetch(own, pieces, weight, sems, shards)
    low_branch = (cot[...].astype(F32) * mod_piece(mod[...], 5, width)).astype(BF16)
    modul = modul_b[...]
    wait_all(copies)
    place = lax.axis_index("shard")
    core = lax.axis_index("replica") % 2
    span = weight.shape[1] // shards
    half = span // 2
    outs = []
    for number in range(shards - 1, -1, -1):
        col = pl.multiple_of((place ^ number) * span, 128)
        pre = dot_nn(modul, weight[:, pl.ds(col, span)]) + bias_fc1[:, pl.ds(col, span)]
        value, rate = gelu_parts(pre)
        value = value.astype(BF16)
        hidden[:, pl.ds(col, span)] = value
        slope[:, pl.ds(col, span)] = rate
        grad[number] = dot_tn(value, low_branch).astype(BF16)
        for side, target in ((core, keep), (1 - core, send)):
            row = pl.multiple_of(side * half, 16)
            copy = pltpu.make_async_copy(
                grad.at[number, pl.ds(row, half), :], target.at[number], out_sems.at[len(outs)]
            )
            copy.start()
            outs.append(copy)
    wait_all(outs)


def pre_kernel(shards, *refs):
    refs = list(refs)
    modul_b, cot, mod, slope = take(refs, 4)
    own = take(refs, 1)
    pieces = take(refs, piece_total(shards))
    low_pre, sum_pre = take(refs, 2)
    keep, send = take(refs, 2)
    weight, grad, turned, sems, out_sems = refs
    rows, width = modul_b.shape
    copies = start_fetch(own, pieces, weight, sems, shards)
    low_branch = (cot[...].astype(F32) * mod_piece(mod[...], 5, width)).astype(BF16)
    turned[...] = modul_b[...].T
    wait_all(copies)

    outs = []
    for col in range(0, weight.shape[0], width):
        cols = slice(col, col + width)
        grad_pre = dot_nt(low_branch, weight[cols, :]) * slope[:, cols]
        sum_pre[:, cols] = jnp.sum(grad_pre, 0, keepdims=True)
        low = grad_pre.astype(BF16)
        low_pre[:, cols] = low
        grad[:, cols] = dot_nn(turned[...], low).astype(BF16)
        start_emit(grad, col, width, keep, send, out_sems, shards, outs)
    wait_all(outs)


def middle_kernel(shards, *refs):
    refs = list(refs)
    low_pre, cot, mod, middle, branch_a = take(refs, 5)
    own = take(refs, 1)
    pieces = take(refs, piece_total(shards))
    grad_middle, low_branch_a, sum_out, grad_mods = take(refs, 4)
    weight, sems = refs
    rows, width = middle.shape
    copies = start_fetch(own, pieces, weight, sems, shards)
    mod_val = mod[...]
    norm_b, rstd_b = layer_norm(middle[...])
    wait_all(copies)
    grad_modul = dot_nt(low_pre[...], weight[...])
    grad_mods[0:1, :] = jnp.sum(grad_modul, 0, keepdims=True)
    grad_mods[1:2, :] = jnp.sum(grad_modul * norm_b, 0, keepdims=True)
    grad_mid = cot[...].astype(F32) + norm_back(
        grad_modul * (1.0 + mod_piece(mod_val, 4, width)), norm_b, rstd_b
    )
    grad_middle[...] = grad_mid
    grad_mods[2:3, :] = jnp.sum(grad_mid * branch_a[...], 0, keepdims=True)
    grad_branch = grad_mid * mod_piece(mod_val, 2, width)
    sum_out[...] = jnp.sum(grad_branch, 0, keepdims=True)
    low_branch_a[...] = grad_branch.astype(BF16)


def back_kernel(shards, *refs):
    refs = list(refs)
    low_branch_a, modul_a, qkv, attended, lse = take(refs, 5)
    own = take(refs, 2)
    pieces = take(refs, piece_total(shards))
    low_proj, sum_proj = take(refs, 2)
    keep, send = take(refs, 2)
    weight, grad, grad_att, turned, sems, out_sems = refs
    rows, width = modul_a.shape
    copies = start_fetch(own, pieces, weight, sems, shards)
    low_branch = low_branch_a[...]
    outs = []
    turned[...] = attended[...].T
    grad[:, 3 * width :] = dot_nn(turned[...], low_branch).astype(BF16)
    start_emit(grad, 3 * width, width, keep, send, out_sems, shards, outs)
    turned[...] = modul_a[...].T
    wait_all(copies)
    grad_att[...] = dot_nt(low_branch, weight[:, 3 * width :]).astype(BF16)
    lane = lax.broadcasted_iota(jnp.int32, (rows, 2 * HEAD), 1)
    lse_val = lse[...]

    def pair(at, carry):
        col = pl.multiple_of(at * 2 * HEAD, 2 * HEAD)
        query = qkv[:, pl.ds(col, 2 * HEAD)]
        key = qkv[:, pl.ds(width + col, 2 * HEAD)]
        value = qkv[:, pl.ds(2 * width + col, 2 * HEAD)]
        grad_out = grad_att[:, pl.ds(col, 2 * HEAD)]
        product = grad_out.astype(F32) * attended[:, pl.ds(col, 2 * HEAD)].astype(F32)
        grad_q = jnp.zeros((rows, 2 * HEAD), F32)
        grad_k = jnp.zeros((rows, 2 * HEAD), F32)
        grad_v = jnp.zeros((rows, 2 * HEAD), F32)
        for side in range(2):
            mask = (lane < HEAD) if side == 0 else (lane >= HEAD)
            query_m = jnp.where(mask, query, 0)
            grad_m = jnp.where(mask, grad_out, 0)
            scores = dot_nt(query_m, key) * 0.125
            log_total = jnp.sum(
                jnp.where(lane == 2 * at + side, lse_val, 0.0), -1, keepdims=True
            )
            probs = jnp.exp(scores - log_total)
            delta = jnp.sum(jnp.where(mask, product, 0.0), -1, keepdims=True)
            grad_scores = (probs * (dot_nt(grad_m, value) - delta) * 0.125).astype(BF16)
            grad_v = grad_v + dot_tn(probs.astype(BF16), grad_m)
            grad_q = grad_q + dot_nn(grad_scores, jnp.where(mask, key, 0))
            grad_k = grad_k + dot_tn(grad_scores, query_m)
        for part, piece in enumerate((grad_q, grad_k, grad_v)):
            there = pl.multiple_of(part * width + col, 2 * HEAD)
            sum_proj[:, pl.ds(there, 2 * HEAD)] = jnp.sum(piece, 0, keepdims=True)
            low_proj[:, pl.ds(there, 2 * HEAD)] = piece.astype(BF16)
        return carry

    lax.fori_loop(0, width // (2 * HEAD), pair, 0, unroll=2)
    for at in range(3):
        cols = slice(at * width, (at + 1) * width)
        grad[:, cols] = dot_nn(turned[...], low_proj[:, cols]).astype(BF16)
        start_emit(grad, at * width, width, keep, send, out_sems, shards, outs)
    wait_all(outs)


def tokens_kernel(shards, *refs):
    refs = list(refs)
    low_proj, tokens, mod, grad_middle = take(refs, 4)
    own = take(refs, 2)
    pieces = take(refs, piece_total(shards))
    grad_tokens, grad_mods = take(refs, 2)
    weight, sems = refs
    rows, width = tokens.shape
    copies = start_fetch(own, pieces, weight, sems, shards)
    norm_a, rstd_a = layer_norm(tokens[...].astype(F32))
    wait_all(copies)
    grad_modul = dot_nt(low_proj[...], weight[:, : 3 * width])
    grad_mods[0:1, :] = jnp.sum(grad_modul, 0, keepdims=True)
    grad_mods[1:2, :] = jnp.sum(grad_modul * norm_a, 0, keepdims=True)
    grad_tokens[...] = grad_middle[...] + norm_back(
        grad_modul * (1.0 + mod_piece(mod[...], 1, width)), norm_a, rstd_a
    )


def mixed_kernel(shards, *refs):
    refs = list(refs)
    hidden, mod, middle, cot, bias_fc2 = take(refs, 5)
    mods_a, mods_b, sum_proj, sum_out, sum_pre = take(refs, 5)
    own = take(refs, 1)
    pieces = take(refs, piece_total(shards))
    mixed, news = take(refs, 2)
    weight, sems = refs
    rows, width = middle.shape
    copies = start_fetch(own, pieces, weight, sems, shards)
    gate_b = mod_piece(mod[...], 5, width)
    grad_out = cot[...].astype(F32)
    wait_all(copies)
    branch_b = dot_nn(hidden[...], weight[...]) + bias_fc2[...]
    mixed[...] = (middle[...] + gate_b * branch_b).astype(BF16)
    sums = [mods_a[0:1, :], mods_a[1:2, :], mods_b[2:3, :], mods_b[0:1, :], mods_b[1:2, :]]
    sums.append(jnp.sum(grad_out * branch_b, 0, keepdims=True))
    sums += [sum_proj[:, :width], sum_proj[:, 2 * width :], sum_out[...], sum_pre[...]]
    sums.append(jnp.sum(grad_out * gate_b, 0, keepdims=True))
    low = 0
    for piece in sums:
        news[:, low : low + piece.shape[1]] = piece.astype(BF16)
        low += piece.shape[1]


def share_kernel(shards, *refs):
    refs = list(refs)
    news = take(refs, shards)
    w_mod, group_cols = take(refs, 2)
    back = take(refs, shards)
    share, rows_ref = refs
    span = w_mod.shape[1]
    cols = w_mod.shape[0]
    rows_ref[...] = jnp.zeros_like(rows_ref)
    biases = jnp.zeros((1, news[0].shape[1] - span), F32)
    for at in range(shards):
        rows_ref[at : at + 1, :span] = news[at][:, :span].astype(F32)
        biases = biases + news[at][:, span:].astype(F32)
    low = rows_ref[:, :span].astype(BF16)
    rows_back = dot_nt(low, w_mod[...])
    for at in range(shards):
        for owner in range(shards):
            back[at][:, owner * cols : (owner + 1) * cols] = jnp.where(
                lax.axis_index("shard") == owner, rows_back[at : at + 1, :], 0.0
            )
    rows_ref[:shards, span : span + cols] = group_cols[...].astype(F32)
    part = biases.shape[1] // 2
    for at in range(2):
        rows_ref[shards + at : shards + at + 1, :part] = biases[:, at * part : (at + 1) * part]
    share[0] = rows_ref[...].astype(BF16)


def total_kernel(shards, *refs):
    share, total_mod, own_mod, own_qv, own_out, own_fc1, own_fc2 = refs
    cols, span = total_mod.shape
    groups, count, _ = share.shape
    row = lax.broadcasted_iota(jnp.int32, (count, 1), 0)
    total = jnp.zeros((count, share.shape[2]), F32)
    for at in range(groups):
        total = total + share[at].astype(F32)
    place = lax.axis_index("shard")

    def own(target, values):
        size = target.shape[0]
        found = jnp.zeros((1, size), F32)
        for at in range(shards):
            found = jnp.where(place == at, values[:, at * size : (at + 1) * size], found)
        target[...] = found[0]

    own(own_mod, jnp.sum(jnp.where(row < shards, total[:, :span], 0.0), 0, keepdims=True))
    part = shards * (own_qv.shape[0] + own_out.shape[0] + own_fc1.shape[0] + own_fc2.shape[0]) // 2
    biases = jnp.concatenate(
        [total[shards : shards + 1, :part], total[shards + 1 : shards + 2, :part]], 1
    )
    low = 0
    for target in (own_qv, own_out, own_fc1, own_fc2):
        high = low + shards * target.shape[0]
        own(target, biases[:, low:high])
        low = high
    whole = share[...].reshape(groups * count, share.shape[2])
    left = whole[:, span : span + cols]
    total_mod[...] = dot_tn(left, whole[:, :span])


def call(kernel, shards, inside, outside, outs, outside_outs, scratch, flops):
    vmem = pl.BlockSpec(memory_space=pltpu.VMEM)
    anywhere = pl.BlockSpec(memory_space=pl.ANY)
    moved = sum(value.size * value.dtype.itemsize for value in inside + outside)
    moved += sum(value.size * value.dtype.itemsize for value in outs + outside_outs)
    return pl.pallas_call(
        functools.partial(kernel, shards),
        out_shape=outs + outside_outs,
        in_specs=[vmem] * len(inside) + [anywhere] * len(outside),
        out_specs=[vmem] * len(outs) + [anywhere] * len(outside_outs),
        scratch_shapes=scratch,
        cost_estimate=pl.CostEstimate(flops=flops, bytes_accessed=moved, transcendentals=0),
        compiler_params=pltpu.CompilerParams(vmem_limit_bytes=56 << 20),
    )(*inside, *outside)


def shape(dims, dtype):
    return jax.ShapeDtypeStruct(dims, dtype)


def body(
    shards,
    replicas,
    tokens,
    cond,
    cot,
    w_mod,
    b_mod,
    w_qkv,
    b_qv,
    w_out,
    b_out,
    w_fc1,
    b_fc1,
    w_fc2,
    b_fc2,
):
    place = lax.axis_index("shard")
    core = lax.axis_index("replica") % 2
    rows, width = tokens.shape
    mod_rows = w_mod.shape[0]
    inner = w_fc1.shape[1]

    def half_of(weight):
        half = weight.shape[0] // 2
        return lax.dynamic_slice_in_dim(weight, core * half, half, 0)

    all_qkvo = Gather(jnp.concatenate([half_of(w_qkv), half_of(w_out)], 1), shards, replicas)
    all_fc1 = Gather(half_of(w_fc1), shards, replicas)
    all_fc2 = Gather(half_of(w_fc2), shards, replicas)
    cond_f = cond.astype(F32)
    cond_act = jax.nn.silu(cond_f).astype(BF16)
    biases = [b_qv, b_out, b_fc1, b_fc2]
    note = jnp.concatenate([cond_act[0]] + biases)[None]
    got = all_qkvo.send(1, all_qkvo.operands(1))
    came = [hop(note, "shard", shards, number) for number in range(1, shards)]
    got = gate(got, *came)
    all_qkvo.hold(1, got)
    notes = jnp.concatenate([note] + gate(came, *got), 0)
    group_cols = lax.dynamic_slice_in_dim(notes[:, :width], place * mod_rows, mod_rows, 1)
    partial = dot_nn(group_cols, w_mod)
    own_bias = lax.dynamic_update_slice(
        jnp.zeros((6 * width,), F32), b_mod.astype(F32), (place * b_mod.shape[0],)
    )
    partial = partial + own_bias
    def rest(gather, behind):
        for depth in range(2, gather.depths + 1):
            got = gather.send(depth, behind if depth == 2 else gather.operands(depth))
            if depth < gather.depths:
                gather.hold(depth, got)
        return got

    came = [hop(partial[number : number + 1], "shard", shards, number) for number in range(1, shards)]
    got = rest(all_qkvo, all_qkvo.operands(2))
    all_qkvo.hold(all_qkvo.depths, got)
    mod = partial[0:1]
    for row in came:
        mod = mod + row
    bias_rows = xor_rows(gate([notes], partial)[0][:, width:].astype(F32), place)
    full_bias = []
    start = 0
    for piece in biases:
        full_bias.append(bias_rows[:, start : start + piece.shape[0]].reshape(1, -1))
        start += piece.shape[0]
    bias_qv, bias_out, bias_fc1, bias_fc2 = full_bias

    pieces_qkvo = all_qkvo.pieces()
    ahead = gate(all_fc1.operands(1), *got)
    got_fc1 = all_fc1.send(1, ahead)
    tokens_in = after(tokens, *ahead)

    pieces = piece_total(shards)
    sems = pltpu.SemaphoreType.DMA
    qkvo_scratch = [pltpu.VMEM((width, 4 * width), BF16)]
    fc1_scratch = [pltpu.VMEM((width, inner), BF16)]
    fc2_scratch = [pltpu.VMEM((inner, width), BF16)]
    half = mod_rows // 2
    half_inner = w_fc2.shape[0] // 2
    chunks = inner // width

    modul_a, qkv, attended, lse, branch_a, middle, modul_b = call(
        attend_kernel,
        shards,
        [tokens_in, mod, bias_qv, bias_out],
        [w_qkv, w_out] + pieces_qkvo,
        [
            shape((rows, width), BF16),
            shape((rows, 3 * width), BF16),
            shape((rows, width), BF16),
            shape((rows, 2 * HEAD), F32),
            shape((rows, width), F32),
            shape((rows, width), F32),
            shape((rows, width), BF16),
        ],
        [],
        qkvo_scratch + [sems((pieces + 2,))],
        10**11,
    )
    got_fc1, [modul_b, middle] = together(got_fc1, [modul_b, middle])
    all_fc1.hold(1, got_fc1)
    got = rest(all_fc1, all_fc1.operands(2))
    ahead = gate(all_fc2.operands(1), *got)
    all_fc1.hold(all_fc1.depths, got)
    pieces_fc1 = all_fc1.pieces()
    got_fc2 = all_fc2.send(1, ahead)
    hidden, slope, *outs = call(
        hidden_kernel,
        shards,
        [after(modul_b, *ahead), cot, mod, bias_fc1],
        [w_fc1] + pieces_fc1,
        [shape((rows, inner), BF16), shape((rows, inner), F32)],
        [shape((shards, half_inner, width), BF16)] * 2,
        fc1_scratch
        + [pltpu.VMEM((shards, 2 * half_inner, width), BF16)]
        + [sems((pieces + 1,)), sems((2 * shards,))],
        10**11,
    )
    got_fc2, [slope, *outs] = together(got_fc2, [slope, *outs])
    all_fc2.hold(1, got_fc2)
    all_fc2.hold(all_fc2.depths, rest(all_fc2, all_fc2.operands(2)))
    pieces_fc2 = all_fc2.pieces()
    red_fc2 = Reduction(outs[0], outs[1], shards, replicas, 1)
    red_fc2.swap()
    stages = len(red_fc2.bits)
    steps = red_fc2.rounds()
    slope = after(slope, *red_fc2.ready(0))
    red_fc2.send(0)
    low_pre, sum_pre, *outs = call(
        pre_kernel,
        shards,
        [modul_b, cot, mod, slope],
        [w_fc2] + pieces_fc2,
        [shape((rows, inner), BF16), shape((1, inner), F32)],
        [shape((shards, half, inner), BF16)] * 2,
        fc2_scratch
        + fc1_scratch
        + [pltpu.VMEM((width, rows), BF16), sems((pieces + 1,)), sems((2 * shards * chunks,))],
        10**11,
    )
    got, [low_pre, *outs] = together(red_fc2.flying, [low_pre, *outs])
    red_fc2.land(got)
    red_fc1 = Reduction(outs[0], outs[1], shards, replicas, 1)
    red_fc1.swap()
    for stage in range(1, stages - 1):
        red_fc2.ready(stage)
        red_fc2.land(red_fc2.send(stage))
    low_pre = after(low_pre, *red_fc2.ready(stages - 1))
    red_fc2.send(stages - 1)
    grad_middle, low_branch_a, sum_out, mods_b = call(
        middle_kernel,
        shards,
        [low_pre, cot, mod, middle, branch_a],
        [w_fc1] + pieces_fc1,
        [
            shape((rows, width), F32),
            shape((rows, width), BF16),
            shape((1, width), F32),
            shape((3, width), F32),
        ],
        [],
        fc1_scratch + [sems((pieces + 1,))],
        10**11,
    )
    got, [red_fc1.came], [low_branch_a] = together(
        red_fc2.flying, [red_fc1.came], [low_branch_a]
    )
    red_fc2.land(got)
    low_branch_a = after(low_branch_a, *red_fc1.ready(0), *red_fc2.own())
    red_fc1.send(0)
    red_fc2.fold(0)
    low_proj, sum_proj, *outs = call(
        back_kernel,
        shards,
        [low_branch_a, modul_a, qkv, attended, lse],
        [w_qkv, w_out] + pieces_qkvo,
        [shape((rows, 3 * width), BF16), shape((1, 3 * width), F32)],
        [shape((shards, half, 4 * width), BF16)] * 2,
        qkvo_scratch
        + qkvo_scratch
        + [pltpu.VMEM((rows, width), BF16), pltpu.VMEM((width, rows), BF16)]
        + [sems((pieces + 2,)), sems((8 * shards,))],
        10**11,
    )
    got_2, got_1, [low_proj, *outs] = together(
        red_fc2.flying, red_fc1.flying, [low_proj, *outs]
    )
    red_fc2.folded(0, got_2)
    red_fc1.land(got_1)
    red_qkvo = Reduction(outs[0], outs[1], shards, replicas, part_count(shards))
    red_qkvo.swap()
    for stage in range(1, stages - 1):
        red_fc1.ready(stage)
        red_fc1.land(red_fc1.send(stage))
    low_proj = after(low_proj, *red_qkvo.ready(0), *red_fc1.ready(stages - 1), *red_fc2.values)
    red_qkvo.send(0)
    red_fc1.send(stages - 1)
    flying_2 = red_fc2.fold(1) if steps > 1 else []
    grad_tokens, mods_a = call(
        tokens_kernel,
        shards,
        [low_proj, tokens, mod, grad_middle],
        [w_qkv, w_out] + pieces_qkvo,
        [shape((rows, width), F32), shape((2, width), F32)],
        [],
        qkvo_scratch + [sems((pieces + 2,))],
        10**11,
    )
    got_q, got_1, got_2, [mods_a] = together(
        red_qkvo.flying, red_fc1.flying, flying_2, [mods_a]
    )
    red_qkvo.land(got_q)
    red_fc1.land(got_1)
    if steps > 1:
        red_fc2.folded(1, got_2)
    for stage in range(1, stages - 1):
        red_qkvo.ready(stage)
        red_qkvo.land(red_qkvo.send(stage))
    sent_q = red_qkvo.ready(stages - 1)
    red_qkvo.send(stages - 1)
    red_fc1.own()
    red_fc1.fold(0)
    flying_2 = red_fc2.fold(2) if steps > 2 else []
    mods_a = after(mods_a, *sent_q, *red_fc1.values, *red_fc2.values)
    mixed, news = call(
        mixed_kernel,
        shards,
        [hidden, mod, middle, cot, bias_fc2, mods_a, mods_b, sum_proj, sum_out, sum_pre],
        [w_fc2] + pieces_fc2,
        [
            shape((rows, width), BF16),
            shape((1, 6 * width + 3 * width + inner + width), BF16),
        ],
        [],
        fc2_scratch + [sems((pieces + 1,))],
        10**11,
    )
    got_q, got_1, got_2, [news] = together(
        red_qkvo.flying, red_fc1.flying, flying_2, [news]
    )
    red_qkvo.land(got_q)
    red_fc1.folded(0, got_1)
    if steps > 2:
        red_fc2.folded(2, got_2)

    red_qkvo.own()

    count = -(-(shards + 2) // 8) * 8
    mod_span = 6 * width
    share_span = mod_span + 2 * 128 * -(-mod_rows // 256)
    share_steps = replicas.bit_length() - 1

    def mod_chain():
        got = yield [(news, "shard", number) for number in range(1, shards)]
        held = [news] + got
        *back, share = call(
            share_kernel,
            shards,
            held + [w_mod, group_cols],
            [],
            [shape((1, width), F32)] * shards + [shape((1, count, share_span), BF16)],
            [],
            [pltpu.VMEM((count, share_span), F32)],
            10**11,
        )
        share, *back = yield [(value, None, 0) for value in [share, *back]]
        rows = dict(enumerate(back))
        step = 0
        while step < share_steps:
            moving = [(share, "replica", replicas >> (step + 1))]
            half = shards >> step if step else 0
            if half:
                moving += [(rows[half + at], "shard", half) for at in range(half)]
            got = yield moving
            share = jnp.concatenate([share, got[0]], 0)
            for at in range(half):
                rows[at] = rows[at] + got[1 + at]
            step += 1
        while shards >> step:
            half = shards >> step
            got = yield [(rows[half + at], "shard", half) for at in range(half)]
            for at in range(half):
                rows[at] = rows[at] + got[at]
            step += 1
        mod_chain.result = (share, rows[0])

    def send_on(moves):
        return [
            hop(value, axis, shards if axis == "shard" else replicas, flip) if axis else value
            for value, axis, flip in moves
        ]

    chain = mod_chain()
    moves = list(next(chain))
    lanes = {red_qkvo: 0, red_fc1: 1, red_fc2: min(3, steps)}
    totals = []
    while chain or min(lanes.values()) < steps:
        moving = [lane for lane in lanes if lanes[lane] < steps]
        groups = [lane.fold(lanes[lane]) for lane in moving]
        *groups, totals = together(*groups, send_on(moves), totals)
        for lane, got in zip(moving, groups):
            lane.folded(lanes[lane], got)
            lanes[lane] += 1
        if moving and min(lanes.values()) == steps:
            whole = red_qkvo.finish()
            totals = [whole[:, : 3 * width], whole[:, 3 * width :]]
        moves = []
        if chain:
            try:
                moves = list(chain.send(groups[-1]))
            except StopIteration:
                chain = None
    share, grad_row = mod_chain.result
    _, silu_back = jax.vjp(jax.nn.silu, cond_f)
    grad_cond = silu_back(grad_row)[0]
    total_mod, total_b_mod, *bias_totals = call(
        total_kernel,
        shards,
        [share],
        [],
        [shape((mod_rows, mod_span), F32), shape(b_mod.shape, F32)]
        + [shape(piece.shape, F32) for piece in biases],
        [],
        [],
        10**8,
    )

    total_fc2 = red_fc2.finish()
    total_fc1 = red_fc1.finish()
    return (
        mixed,
        grad_tokens,
        grad_cond,
        total_mod,
        total_b_mod,
        totals[0],
        bias_totals[0],
        totals[1],
        bias_totals[1],
        total_fc1,
        bias_totals[2],
        total_fc2,
        bias_totals[3],
    )


def solution(mesh):
    shards = mesh.shape["shard"]
    replicas = mesh.shape["replica"]
    both = P(("shard", "replica"), None)
    pairs = (P("shard", None), P("shard")) * 5

    def run(*args):
        return body(shards, replicas, *args)

    return jax.shard_map(
        run,
        mesh=mesh,
        in_specs=(both, both, both) + pairs,
        out_specs=(both, both, both) + pairs,
        check_vma=False,
    )
```
